256 devices in a mesh: grp: 128 (over z, x, y), rep: 2 (over core).
Axes of the slice: x: 4, y: 4, z: 8, core: 2. Of those that a mesh axis runs over, the one named last changes fastest.
Arguments:
- snapshots: float32 [128, 2048, 1024], P('grp', 'rep'), may hold values from -6 to 6
- row_factor: float32 [2048, 128], P('rep'), may hold values from -0.125 to 0.125
- time_factor: float32 [128, 64], replicated, may hold values from -0.5 to 0.5
Outputs:
- new_rows: float32 [2048, 128], P('rep')
- new_time: float32 [128, 64], replicated
The draws below stay inside these ranges and needn't reach their ends.
All inputs are finite; a program needn't handle non-finite values.
Results may differ from the reference program's by a relative error of at most 0.0001.
Values sent between devices are 32-bit elements; how exact they have to be, the bound alone decides.
A program may use at most 64 MiB of HBM per device.

```python
import math
import jax
import jax.numpy as jnp
from jax import lax

ROWS = 2048
COLS = 1024
RANK_ROW = 128
STEPS = 8
SNAPS = 128
RANK_TIME = 64


def steps_of(key, dims, cuts, low, high):
    gain, own = 1.0, jax.random.fold_in(key, 6)
    for dim, shards_of in cuts:
        draws = jnp.exp(jax.random.uniform(jax.random.fold_in(own, dim), (shards_of,), jnp.float32, low / len(cuts), high / len(cuts)))
        gain = gain * jnp.repeat(draws, dims[dim] // shards_of).reshape([-1 if axis == dim else 1 for axis in range(len(dims))])
    return gain


def normal_values(own_key, shape, deviation, limit, shards=(), held_as=jnp.bfloat16):
    factor_of = steps_of(own_key, shape, shards, -0.22, 0.18) if shards else 1.0
    entries = jax.random.normal(own_key, shape, jnp.float32) * deviation * factor_of
    return jnp.minimum(jnp.maximum(entries, -limit), limit).astype(held_as)


def setup_inputs(seed: int = 0) -> dict:
    splits = jax.random.split(jax.random.key(seed), 4)
    return {
        "snapshots": normal_values(splits[0], (SNAPS, ROWS, COLS), 1.0, 6.0, ((0, 128), (1, 2)), jnp.float32),
        "row_factor": normal_values(splits[1], (ROWS, RANK_ROW), ROWS ** -0.5, 0.125, ((0, 2),), jnp.float32),
        "time_factor": normal_values(splits[2], (SNAPS, RANK_TIME), SNAPS ** -0.5, 0.5, (), jnp.float32),
    }


def highdot(left, right):
    return jnp.dot(left, right, precision=lax.Precision.HIGHEST, preferred_element_type=jnp.float32)

def orthogonalize(start_matrix):
    total = jnp.sum(start_matrix * start_matrix)
    iterate = start_matrix / jnp.sqrt(total + 1e-06)
    for step_index in range(STEPS):
        inner = highdot(iterate.T, iterate)
        iterate = 1.5 * iterate - 0.5 * highdot(iterate, inner)
    return iterate

def reference(snapshots, row_factor, time_factor):
    projected = jnp.einsum('tij,ia->tja', snapshots, row_factor, precision=lax.Precision.HIGHEST)
    flat = projected.reshape(SNAPS, COLS * RANK_ROW)
    gram_total = jnp.dot(flat, flat.T, precision=lax.Precision.HIGHEST, preferred_element_type=jnp.float32)
    start_time = highdot(gram_total, time_factor)
    basis_time = orthogonalize(start_time)
    mixer = highdot(basis_time, basis_time.T)
    weights = highdot(mixer, flat).reshape(SNAPS, COLS, RANK_ROW)
    product = jnp.einsum('tij,tja->ia', snapshots, weights, precision=lax.Precision.HIGHEST)
    new_rows = orthogonalize(product) * math.sqrt(ROWS)
    new_time = basis_time * math.sqrt(SNAPS)
    return (new_rows, new_time)
```

```python
import functools
import math

import jax
import jax.numpy as jnp
from jax import lax
from jax.experimental import pallas as pl
from jax.experimental.pallas import tpu as pltpu
from jax.sharding import PartitionSpec as P

MESH = pl.DeviceIdType.MESH
STEPS = 8
ZS = 8
F32 = jnp.float32
BF16 = jnp.bfloat16
NN = (((1,), (0,)), ((), ()))
NT = (((1,), (1,)), ((), ()))


def full(left, right, dims=NN):
    return lax.dot_general(left, right, dims, precision=lax.Precision.HIGHEST, preferred_element_type=F32)


def half(left, right, dims=NN):
    return lax.dot_general(left, right, dims, preferred_element_type=F32)


def split(value):
    high = value.astype(BF16)
    return high, (value - high.astype(F32)).astype(BF16)


def pair(first, second):
    upper = lax.broadcasted_iota(jnp.int32, first.shape, 0) < 4
    return (
        jnp.where(upper, first, pltpu.roll(second, 4, 0)),
        jnp.where(upper, pltpu.roll(first, 4, 0), second),
    )


def kernel(nz, snap_ref, row_ref, time_ref, rows_out, time_out,
           snap, shigh, slow, proj, other, piece, plane_in, zsend, owned,
           tpart, tother, tchip, tz, tsum, tplane, tall,
           wback, wz, wsend, wpieces, whigh, wlow,
           prod, pin, psum, pz, xall, gpart, gother,
           load_sem, core_s, core_r, plane_s, plane_r, z_s, z_r):
    count = lax.axis_size("grp")
    nplane = count // nz
    me = lax.axis_index("grp")
    rep = lax.axis_index("rep")
    zi, pi = me // nplane, me % nplane
    sibling = 1 - rep
    rank = row_ref.shape[1]
    rhalf = rank // 2
    rows, cols = snap.shape
    lanes = nz * 64
    per_row = cols // lanes
    chunk = cols // 2
    depth = min(rows, 256)

    loads = []
    for h in range(2):
        cut = pl.ds(h * chunk, chunk)
        load = pltpu.make_async_copy(snap_ref.at[0, :, cut], snap.at[:, cut], load_sem.at[h])
        load.start()
        loads.append(load)

    barrier = pltpu.get_barrier_semaphore()

    def greet(grp, core):
        pl.semaphore_signal(barrier, inc=1, device_id=(grp, core), device_id_type=MESH)

    greet(me, sibling)
    for d in range(1, nz):
        greet(((zi + d) % nz) * nplane + pi, rep)
    for d in range(1, nplane):
        greet(zi * nplane + (pi + d) % nplane, rep)

    def to_core(stage, src, dst):
        copy = pltpu.make_async_remote_copy(
            src_ref=src, dst_ref=dst, send_sem=core_s.at[stage], recv_sem=core_r.at[stage],
            device_id=(me, sibling), device_id_type=MESH)
        copy.start()
        return copy

    def along_z(stage, src, dst):
        copies = []
        for d in range(1, nz):
            q = (zi + d) % nz
            copy = pltpu.make_async_remote_copy(
                src_ref=src(q), dst_ref=dst, send_sem=z_s.at[stage, d], recv_sem=z_r.at[stage, d],
                device_id=(q * nplane + pi, rep), device_id_type=MESH)
            copy.start()
            copies.append(copy)
        return copies

    def in_plane(stage, src, dst):
        copies = []
        for d in range(1, nplane):
            q = (pi + d) % nplane
            copy = pltpu.make_async_remote_copy(
                src_ref=src(q), dst_ref=dst, send_sem=plane_s.at[stage, d], recv_sem=plane_r.at[stage, d],
                device_id=(zi * nplane + q, rep), device_id_type=MESH)
            copy.start()
            copies.append(copy)
        return copies

    started = []

    def arrive(copies):
        for copy in copies:
            copy.wait_recv()
        started.extend(copies)

    uhigh, ulow = split(row_ref[...].T)
    core_copies = []
    for h in range(2):
        loads[h].wait()
        total = jnp.zeros((rank, chunk), F32)
        for k in range(0, rows, depth):
            high, low = split(snap[k:k + depth, h * chunk:(h + 1) * chunk])
            shigh[k:k + depth, h * chunk:(h + 1) * chunk] = high
            slow[k:k + depth, h * chunk:(h + 1) * chunk] = low
            uh, ul = uhigh[:, k:k + depth], ulow[:, k:k + depth]
            total = total + (half(uh, high) + (half(ul, high) + half(uh, low)))
        proj[:, h * chunk:(h + 1) * chunk] = total
        if h == 0:
            pl.semaphore_wait(barrier, nz + nplane - 1)
        cut = pl.ds(h * chunk, chunk)
        core_copies.append(to_core(h, proj.at[pl.ds(sibling * rhalf, rhalf), cut], other.at[:, cut]))
    arrive(core_copies)
    for q in range(nplane):
        at, lo = (q // per_row) * 8, (q % per_row) * lanes
        piece[q] = proj[pl.ds(rep * rhalf + at, 8), lo:lo + lanes] + other[at:at + 8, lo:lo + lanes]

    copies = in_plane(0, lambda q: piece.at[q], plane_in.at[pi])
    plane_in[pi] = piece[pi]
    arrive(copies)
    for t in range(nz // 2):
        for m in range(nplane // 2):
            even, odd = pair(plane_in[2 * m, :, t * 128:(t + 1) * 128], plane_in[2 * m + 1, :, t * 128:(t + 1) * 128])
            zsend[2 * t, m * 8:m * 8 + 8, :] = even
            zsend[2 * t + 1, m * 8:m * 8 + 8, :] = odd
    zrows = nplane * 4
    mine = pl.ds(zi * zrows, zrows)
    copies = along_z(0, lambda q: zsend.at[q], owned.at[mine])
    owned[mine, :] = zsend[zi]
    arrive(copies)
    flat = jnp.concatenate([owned[pl.ds(c, count, stride=4), :] for c in range(4)], axis=1)

    tpart[...] = full(full(time_ref[...], flat), flat, NT)
    swap = to_core(2, tpart, tother)
    arrive([swap])
    tchip[...] = tpart[...] + tother[...]
    trows = tchip.shape[0] // nz
    copies = along_z(1, lambda q: tchip.at[pl.ds(q * trows, trows)], tz.at[zi])
    tz[zi] = tchip[pl.ds(zi * trows, trows), :]
    arrive(copies)
    tsum[...] = functools.reduce(jnp.add, [tz[k] for k in range(nz)])
    copies = in_plane(1, lambda q: tsum, tplane.at[pi])
    tplane[pi] = tsum[...]
    arrive(copies)
    tmine = pl.ds(zi * trows, trows)
    tall[tmine, :] = functools.reduce(jnp.add, [tplane[k] for k in range(nplane)])
    copies = along_z(2, lambda q: tall.at[tmine], tall.at[tmine])
    arrive(copies)
    start = tall[...]

    scale = 1.0 / jnp.sqrt(jnp.sum(start * start, axis=(0, 1), keepdims=True) + 1e-06)

    def time_step(_, basis):
        return 1.5 * basis - 0.5 * full(full(basis, basis, NT), basis)

    basis = lax.fori_loop(0, STEPS, time_step, start * scale)
    time_out[...] = basis * math.sqrt(count)
    mixed = full(full(basis.T, basis), flat)
    for c in range(4):
        wback[pl.ds(c, count, stride=4), :] = mixed[:, c * 128:(c + 1) * 128]

    copies = along_z(3, lambda q: wback.at[pl.ds(q * zrows, zrows)], wz.at[zi])
    wz[zi] = wback[mine, :]
    arrive(copies)
    for t in range(nz // 2):
        for m in range(nplane // 2):
            even, odd = pair(wz[2 * t, m * 8:m * 8 + 8, :], wz[2 * t + 1, m * 8:m * 8 + 8, :])
            wsend[2 * m, :, t * 128:(t + 1) * 128] = even
            wsend[2 * m + 1, :, t * 128:(t + 1) * 128] = odd
    copies = in_plane(2, lambda q: wsend.at[q], wpieces.at[rep, pi])
    wpieces[rep, pi] = wsend[pi]
    arrive(copies)
    swap = to_core(3, wpieces.at[rep], wpieces.at[rep])
    arrive([swap])
    for core in range(2):
        for k in range(rhalf // 16):
            for h in range(per_row):
                block = jnp.concatenate(
                    [wpieces[core, 2 * k * per_row + h], wpieces[core, (2 * k + 1) * per_row + h]], axis=0)
                high, low = split(block)
                at, lo = core * rhalf + k * 16, h * lanes
                whigh[at:at + 16, lo:lo + lanes] = high
                wlow[at:at + 16, lo:lo + lanes] = low

    for k in range(0, rows, depth):
        high, low = shigh[k:k + depth, :], slow[k:k + depth, :]
        prod[k:k + depth, :] = half(high, whigh[...], NT) + (half(high, wlow[...], NT) + half(low, whigh[...], NT))

    prows = rows // nplane
    copies = in_plane(3, lambda q: prod.at[pl.ds(q * prows, prows)], pin.at[pi])
    pin[pi] = prod[pl.ds(pi * prows, prows), :]
    arrive(copies)
    psum[...] = functools.reduce(jnp.add, [pin[k] for k in range(nplane)])
    copies = along_z(4, lambda q: psum.at[pl.ds(q * 8, 8)], pz.at[zi])
    pz[zi] = psum[pl.ds(zi * 8, 8), :]
    arrive(copies)
    xmine = pl.ds(pi * prows + zi * 8, 8)
    xall[xmine, :] = functools.reduce(jnp.add, [pz[k] for k in range(nz)])
    copies = along_z(5, lambda q: xall.at[xmine], xall.at[xmine])
    arrive(copies)
    xplane = pl.ds(pi * prows, prows)
    copies = in_plane(4, lambda q: xall.at[xplane], xall.at[xplane])
    arrive(copies)

    whole = xall[...]
    gpart[...] = full(whole.T, whole)
    swap = to_core(4, gpart, gother)
    arrive([swap])
    gram = gpart[...] + gother[...]
    eye = jnp.where(
        lax.broadcasted_iota(jnp.int32, gram.shape, 0) == lax.broadcasted_iota(jnp.int32, gram.shape, 1), 1.0, 0.0
    ).astype(F32)
    norm = 1.0 / (jnp.sum(gram * eye, axis=(0, 1), keepdims=True) + 1e-06)

    def row_step(_, carry):
        inner, power = carry
        factor = 1.5 * eye - 0.5 * inner
        return full(factor, full(factor, inner)), full(factor, power)

    inner, power = gram * norm, eye
    for k in range(STEPS - 1):
        inner, power = row_step(k, (inner, power))
    power = full(power, 1.5 * eye - 0.5 * inner)
    rows_out[...] = full(whole, power * (math.sqrt(2 * rows) * jnp.sqrt(norm)))
    for copy in started:
        copy.wait_send()


def solution(mesh):
    count = mesh.shape["grp"]
    nz = ZS
    nplane = count // nz

    def on_device(snapshots, row_factor, time_factor):
        _, rows, cols = snapshots.shape
        rank = row_factor.shape[1]
        modes = time_factor.shape[1]
        lanes = nz * 64
        vmem = lambda *shape: pltpu.VMEM(shape, F32)
        narrow = lambda *shape: pltpu.VMEM(shape, BF16)
        sems = lambda *shape: pltpu.SemaphoreType.DMA(shape)
        prows = rows // nplane
        new_rows, new_time = pl.pallas_call(
            functools.partial(kernel, nz),
            out_shape=(
                jax.ShapeDtypeStruct((rows, rank), F32),
                jax.ShapeDtypeStruct((modes, count), F32),
            ),
            in_specs=[
                pl.BlockSpec(memory_space=pltpu.HBM),
                pl.BlockSpec(memory_space=pltpu.VMEM),
                pl.BlockSpec(memory_space=pltpu.VMEM),
            ],
            out_specs=(pl.BlockSpec(memory_space=pltpu.VMEM),) * 2,
            scratch_shapes=[
                vmem(rows, cols), narrow(rows, cols), narrow(rows, cols),
                vmem(rank, cols), vmem(rank // 2, cols),
                vmem(nplane, 8, lanes), vmem(nplane, 8, lanes),
                vmem(nz, nplane * 4, 128), vmem(count * 4, 128),
                vmem(modes, count), vmem(modes, count), vmem(modes, count),
                vmem(nz, modes // nz, count), vmem(modes // nz, count),
                vmem(nplane, modes // nz, count), vmem(modes, count),
                vmem(count * 4, 128), vmem(nz, nplane * 4, 128),
                vmem(nplane, 8, lanes), vmem(2, nplane, 8, lanes),
                narrow(rank, cols), narrow(rank, cols),
                vmem(rows, rank), vmem(nplane, prows, rank), vmem(prows, rank),
                vmem(nz, 8, rank), vmem(rows, rank), vmem(rank, rank), vmem(rank, rank),
                sems(2), sems(5), sems(5), sems(5, nplane), sems(5, nplane), sems(6, nz), sems(6, nz),
            ],
            compiler_params=pltpu.CompilerParams(
                collective_id=0, has_side_effects=True, vmem_limit_bytes=40 * 1024 * 1024),
        )(snapshots, row_factor, time_factor.T)
        return new_rows, new_time.T

    return jax.shard_map(
        on_device,
        mesh=mesh,
        in_specs=(P("grp", "rep", None), P("rep", None), P()),
        out_specs=(P("rep", None), P()),
        check_vma=False,
    )
```

```python
import functools
import math

import jax
import jax.numpy as jnp
from jax import lax
from jax.experimental import pallas as pl
from jax.experimental.pallas import tpu as pltpu
from jax.sharding import PartitionSpec as P

MESH = pl.DeviceIdType.MESH
STEPS = 8
DIMS = (8, 4, 4)
SPREAD = 37
PARTS = 4
VMEM_MIB = 60
F32 = jnp.float32
BF16 = jnp.bfloat16
NN = (((1,), (0,)), ((), ()))
NT = (((1,), (1,)), ((), ()))


def full(left, right, dims=NN):
    return lax.dot_general(left, right, dims, precision=lax.Precision.HIGHEST, preferred_element_type=F32)


def half(left, right, dims=NN):
    return lax.dot_general(left, right, dims, preferred_element_type=F32)


def split(value):
    high = value.astype(BF16)
    return high, (value - high.astype(F32)).astype(BF16)


def kernel(dims, snap_ref, row_ref, time_ref, rows_out, time_out,
           snap, ufac, tfac, shigh, slow, proj, other, piece, owned,
           tpart, tother, tchip, tz, tsum, tplane, tall,
           wback, wpieces, whigh, wlow,
           prod, pin, psum, pz, xall, gpart, gother,
           load_sem, core_s, core_r, plane_s, plane_r, z_s, z_r, all_s, all_r):
    nz, nx, ny = dims
    nplane = nx * ny
    count = nz * nplane
    me = lax.axis_index("grp")
    rep = lax.axis_index("rep")
    zi, pi = me // nplane, me % nplane
    sibling = 1 - rep
    rank = ufac.shape[1]
    rhalf = rank // 2
    rows, cols = snap.shape
    tiles = ny // 2
    width = tiles * 128
    block = nz * ny * 4
    depth = min(rows, 256)

    loads = [pltpu.make_async_copy(row_ref, ufac, load_sem.at[nx]), pltpu.make_async_copy(time_ref, tfac, load_sem.at[nx + 1])]
    for c in range(nx):
        cut = pl.ds(c * width, width)
        loads.append(pltpu.make_async_copy(snap_ref.at[0, :, cut], snap.at[:, cut], load_sem.at[c]))
    for load in loads:
        load.start()

    barrier = pltpu.get_barrier_semaphore()

    def greet(grp, core):
        pl.semaphore_signal(barrier, inc=1, device_id=(grp, core), device_id_type=MESH)

    def greet_one(d, carry):
        greet((me + d * SPREAD) % count, rep)
        return carry

    greet(me, sibling)
    lax.fori_loop(1, count, greet_one, 0)

    started = []

    def begin(copy):
        copy.start()
        started.append(copy)
        return copy

    def to_core(stage, src, dst):
        return [begin(pltpu.make_async_remote_copy(
            src_ref=src, dst_ref=dst, send_sem=core_s.at[stage], recv_sem=core_r.at[stage],
            device_id=(me, sibling), device_id_type=MESH))]

    def along_z(stage, src, dst):
        return [begin(pltpu.make_async_remote_copy(
            src_ref=src, dst_ref=dst, send_sem=z_s.at[stage, d], recv_sem=z_r.at[stage, d],
            device_id=((zi + d) % nz * nplane + pi, rep), device_id_type=MESH)) for d in range(1, nz)]

    def in_plane(stage, src, dst):
        copies = []
        for d in range(1, nplane):
            q = (pi + d) % nplane
            copies.append(begin(pltpu.make_async_remote_copy(
                src_ref=src(q), dst_ref=dst, send_sem=plane_s.at[stage, d], recv_sem=plane_r.at[stage, d],
                device_id=(zi * nplane + q, rep), device_id_type=MESH)))
        return copies

    def arrive(copies):
        for copy in copies:
            copy.wait_recv()

    def place(grp):
        z, x, y = grp // nplane, grp % nplane // ny, grp % ny
        return (x + z) % nx * block + z * (ny * 4) + y * 4

    def to_owner(stage, src, dst, grp):
        return pltpu.make_async_remote_copy(
            src_ref=src, dst_ref=dst, send_sem=all_s.at[stage], recv_sem=all_r.at[stage],
            device_id=(grp, rep), device_id_type=MESH)

    loads[0].wait()
    uhigh, ulow = split(ufac[...].T)
    core_copies = []
    for c in range(nx):
        loads[2 + c].wait()
        lo = c * width
        total = jnp.zeros((rank, width), F32)
        for k in range(0, rows, depth):
            high, low = split(snap[k:k + depth, lo:lo + width])
            shigh[k:k + depth, lo:lo + width] = high
            slow[k:k + depth, lo:lo + width] = low
            uh, ul = uhigh[:, k:k + depth], ulow[:, k:k + depth]
            total = total + (half(uh, high) + (half(ul, high) + half(uh, low)))
        for core in range(2):
            for z in range(nz):
                for k in range(tiles):
                    at = c * block + z * ny * 4 + k * 8
                    proj[core, at:at + 8, :] = total[core * rhalf + z * 8:core * rhalf + z * 8 + 8, k * 128:k * 128 + 128]
        if c == 0:
            pl.semaphore_wait(barrier, count)
        cut = pl.ds(c * block, block)
        core_copies.append(to_core(c, proj.at[sibling, cut], other.at[cut]))

    for c in range(nx):
        arrive(core_copies[c])
        at = c * block
        piece[at:at + block, :] = proj[rep, at:at + block, :] + other[at:at + block, :]

        def send(u, carry):
            v = (u * 5 + zi * ny + pi % ny) % (nz * ny)
            z, y = v // ny, v % ny
            grp = z * nplane + (c + nx * nz - z) % nx * ny + y

            @pl.when(grp != me)
            def _():
                to_owner(0, piece.at[pl.ds(at + z * (ny * 4) + y * 4, 4)], owned.at[pl.ds(me * 4, 4)], grp).start()

            return carry

        lax.fori_loop(0, nz * ny, send, 0)
    pltpu.make_async_copy(piece.at[pl.ds(place(me), 4)], owned.at[pl.ds(me * 4, 4)], all_r.at[0]).start()
    pltpu.make_async_copy(owned, owned, all_r.at[0]).wait()
    flat = jnp.concatenate([owned[pl.ds(c, count, stride=4), :] for c in range(4)], axis=1)

    loads[1].wait()
    tpart[...] = full(full(tfac[...], flat), flat, NT)
    thalf = tpart.shape[0] // 2
    tmine = pl.ds(rep * thalf, thalf)
    arrive(to_core(nx, tpart.at[pl.ds(sibling * thalf, thalf)], tother))
    tchip[...] = tpart[tmine, :] + tother[...]
    copies = along_z(0, tchip, tz.at[zi])
    tz[zi] = tchip[...]
    arrive(copies)
    tsum[...] = functools.reduce(jnp.add, [tz[k] for k in range(nz)])
    copies = in_plane(0, lambda q: tsum, tplane.at[pi])
    tplane[pi] = tsum[...]
    arrive(copies)
    tall[tmine, :] = functools.reduce(jnp.add, [tplane[k] for k in range(nplane)])
    arrive(to_core(nx + 1, tall.at[tmine], tall.at[tmine]))
    start = tall[...]

    scale = 1.0 / jnp.sqrt(jnp.sum(start * start, axis=(0, 1), keepdims=True) + 1e-06)

    def time_step(_, basis):
        return 1.5 * basis - 0.5 * full(full(basis, basis, NT), basis)

    basis = lax.fori_loop(0, STEPS, time_step, start * scale)
    time_out[...] = basis * math.sqrt(count)
    mixed = full(full(basis.T, basis), flat)
    for c in range(4):
        wback[pl.ds(c, count, stride=4), :] = mixed[:, c * 128:(c + 1) * 128]

    spot = pl.ds(place(me), 4)

    def send_back(d, carry):
        grp = (me + d * SPREAD) % count
        to_owner(1, wback.at[pl.ds(grp * 4, 4)], wpieces.at[rep, spot], grp).start()
        return carry

    lax.fori_loop(1, count, send_back, 0)
    pltpu.make_async_copy(wback.at[pl.ds(me * 4, 4)], wpieces.at[rep, spot], all_r.at[1]).start()
    pltpu.make_async_copy(wback, wback, all_r.at[1]).wait()
    arrive(to_core(nx + 2, wpieces.at[rep], wpieces.at[rep]))
    for core in range(2):
        for m in range(nz // 2):
            for c in range(nx):
                for k in range(tiles):
                    at = c * block + 2 * m * ny * 4 + k * 8
                    both = jnp.concatenate(
                        [wpieces[core, at:at + 8, :], wpieces[core, at + ny * 4:at + ny * 4 + 8, :]], axis=0)
                    high, low = split(both)
                    row, lo = core * rhalf + m * 16, c * width + k * 128
                    whigh[row:row + 16, lo:lo + 128] = high
                    wlow[row:row + 16, lo:lo + 128] = low

    part = rows // PARTS
    prows = part // nplane
    summed, crossed, spread = [], [], []
    for h in range(PARTS):
        for k in range(h * part, (h + 1) * part, min(part, 256)):
            high, low = shigh[k:k + min(part, 256), :], slow[k:k + min(part, 256), :]
            prod[k:k + min(part, 256), :] = half(high, whigh[...], NT) + (
                half(high, wlow[...], NT) + half(low, whigh[...], NT))
        summed.append(in_plane(1 + h, lambda q: prod.at[pl.ds(h * part + q * prows, prows)], pin.at[h, pi]))
        pin[h, pi] = prod[pl.ds(h * part + pi * prows, prows), :]
    for h in range(PARTS):
        arrive(summed[h])
        psum[h] = functools.reduce(jnp.add, [pin[h, k] for k in range(nplane)])
        crossed.append(along_z(1 + h, psum.at[h], pz.at[h, zi]))
        pz[h, zi] = psum[h]
    for h in range(PARTS):
        arrive(crossed[h])
        mine = pl.ds(h * part + pi * prows, prows)
        xall[mine, :] = functools.reduce(jnp.add, [pz[h, k] for k in range(nz)])
        spread.append(in_plane(1 + PARTS + h, lambda q: xall.at[mine], xall.at[mine]))
    gram = jnp.zeros((rank, rank), F32)
    for h in range(PARTS):
        arrive(spread[h])
        some = xall[h * part:(h + 1) * part, :]
        gram = gram + full(some.T, some)
    gpart[...] = gram
    arrive(to_core(nx + 3, gpart, gother))
    gram = gpart[...] + gother[...]

    eye = jnp.where(
        lax.broadcasted_iota(jnp.int32, gram.shape, 0) == lax.broadcasted_iota(jnp.int32, gram.shape, 1), 1.0, 0.0
    ).astype(F32)
    norm = 1.0 / (jnp.sum(gram * eye, axis=(0, 1), keepdims=True) + 1e-06)
    inner, power = gram * norm, eye
    for _ in range(STEPS - 1):
        factor = 1.5 * eye - 0.5 * inner
        inner, power = full(factor, full(factor, inner)), full(factor, power)
    power = full(power, 1.5 * eye - 0.5 * inner)
    rows_out[...] = full(xall[...], power * (math.sqrt(2 * rows) * jnp.sqrt(norm)))
    for copy in started:
        copy.wait_send()
    rest = pl.ds(0, (count - 1) * 4)
    for stage in range(2):
        pltpu.make_async_copy(owned.at[rest], owned.at[rest], all_s.at[stage]).wait()


def solution(mesh):
    nz, nx, ny = dims = DIMS
    nplane = nx * ny
    count = nz * nplane

    def on_device(snapshots, row_factor, time_factor):
        _, rows, cols = snapshots.shape
        rank = row_factor.shape[1]
        modes = time_factor.shape[1]
        vmem = lambda *shape: pltpu.VMEM(shape, F32)
        narrow = lambda *shape: pltpu.VMEM(shape, BF16)
        sems = lambda *shape: pltpu.SemaphoreType.DMA(shape)
        part = rows // PARTS
        prows = part // nplane
        new_rows, new_time = pl.pallas_call(
            functools.partial(kernel, dims),
            out_shape=(
                jax.ShapeDtypeStruct((rows, rank), F32),
                jax.ShapeDtypeStruct((modes, count), F32),
            ),
            in_specs=[pl.BlockSpec(memory_space=pltpu.HBM)] * 3,
            out_specs=(pl.BlockSpec(memory_space=pltpu.VMEM),) * 2,
            scratch_shapes=[
                vmem(rows, cols), vmem(rows, rank), vmem(modes, count), narrow(rows, cols), narrow(rows, cols),
                vmem(2, count * 4, 128), vmem(count * 4, 128), vmem(count * 4, 128), vmem(count * 4, 128),
                vmem(modes, count), vmem(modes // 2, count), vmem(modes // 2, count),
                vmem(nz, modes // 2, count), vmem(modes // 2, count),
                vmem(nplane, modes // 2, count), vmem(modes, count),
                vmem(count * 4, 128), vmem(2, count * 4, 128),
                narrow(rank, cols), narrow(rank, cols),
                vmem(rows, rank), vmem(PARTS, nplane, prows, rank), vmem(PARTS, prows, rank),
                vmem(PARTS, nz, prows, rank), vmem(rows, rank), vmem(rank, rank), vmem(rank, rank),
                sems(nx + 2), sems(nx + 4), sems(nx + 4), sems(1 + 2 * PARTS, nplane), sems(1 + 2 * PARTS, nplane),
                sems(1 + PARTS, nz), sems(1 + PARTS, nz), sems(2), sems(2),
            ],
            compiler_params=pltpu.CompilerParams(
                collective_id=0, has_side_effects=True, vmem_limit_bytes=VMEM_MIB * 1024 * 1024),
        )(snapshots, row_factor, time_factor.T)
        return new_rows, new_time.T

    return jax.shard_map(
        on_device,
        mesh=mesh,
        in_specs=(P("grp", "rep", None), P("rep", None), P()),
        out_specs=(P("rep", None), P()),
        check_vma=False,
    )
```

```python
import functools
import math

import jax
import jax.numpy as jnp
from jax import lax
from jax.experimental import pallas as pl
from jax.experimental.pallas import tpu as pltpu
from jax.sharding import PartitionSpec as P

MESH = pl.DeviceIdType.MESH
STEPS = 8
DIMS = (8, 4, 4)
PARTS = 4
VMEM_MIB = 40
F32 = jnp.float32
BF16 = jnp.bfloat16
NN = (((1,), (0,)), ((), ()))
NT = (((1,), (1,)), ((), ()))


def full(left, right, dims=NN):
    return lax.dot_general(left, right, dims, precision=lax.Precision.HIGHEST, preferred_element_type=F32)


def half(left, right, dims=NN):
    return lax.dot_general(left, right, dims, preferred_element_type=F32)


def split(value):
    high = value.astype(BF16)
    return high, (value - high.astype(F32)).astype(BF16)


def kernel(dims, snap_ref, row_ref, time_ref, rows_out, time_out,
           snap, ufac, tfac, shigh, slow, proj, other, piece, owned,
           tpart, tother, tchip, trows, tsum, tall,
           wback, wpieces, whigh, wlow,
           prod, pin, psum, pz, xall, gpart, gother,
           load_sem, core_s, core_r, plane_s, plane_r, z_s, z_r, all_s, all_r, word_sem):
    nz, nx, ny = dims
    nplane = nx * ny
    count = nz * nplane
    me = lax.axis_index("grp")
    rep = lax.axis_index("rep")
    zi, pi = me // nplane, me % nplane
    sibling = 1 - rep
    rank = ufac.shape[1]
    rhalf = rank // 2
    rows, cols = snap.shape
    tiles = ny // 2
    width = tiles * 128
    block = nz * ny * 4
    depth = min(rows, 256)

    loads = [pltpu.make_async_copy(row_ref, ufac, load_sem.at[nx]), pltpu.make_async_copy(time_ref, tfac, load_sem.at[nx + 1])]
    for c in range(nx):
        cut = pl.ds(c * width, width)
        loads.append(pltpu.make_async_copy(snap_ref.at[0, :, cut], snap.at[:, cut], load_sem.at[c]))
    for load in loads:
        load.start()

    barrier = pltpu.get_barrier_semaphore()

    def greet(grp, core):
        pl.semaphore_signal(barrier, inc=1, device_id=(grp, core), device_id_type=MESH)

    greet(me, sibling)
    for d in range(1, nz):
        greet((zi + d) % nz * nplane + pi, rep)
    for d in range(1, nplane):
        greet(zi * nplane + (pi + d) % nplane, rep)
    pl.semaphore_wait(barrier, nz + nplane - 1)
    for d in range(1, nz):
        pl.semaphore_signal(
            word_sem, inc=1, device_id=((zi + d) % nz * nplane + pi, rep), device_id_type=MESH)

    started = []

    def begin(copy):
        copy.start()
        started.append(copy)
        return copy

    def to_core(stage, src, dst):
        return [begin(pltpu.make_async_remote_copy(
            src_ref=src, dst_ref=dst, send_sem=core_s.at[stage], recv_sem=core_r.at[stage],
            device_id=(me, sibling), device_id_type=MESH))]

    def along_z(stage, src, dst):
        return [begin(pltpu.make_async_remote_copy(
            src_ref=src, dst_ref=dst, send_sem=z_s.at[stage, d], recv_sem=z_r.at[stage, d],
            device_id=((zi + d) % nz * nplane + pi, rep), device_id_type=MESH)) for d in range(1, nz)]

    def in_plane(stage, src, dst):
        copies = []
        for d in range(1, nplane):
            q = (pi + d) % nplane
            copies.append(begin(pltpu.make_async_remote_copy(
                src_ref=src(q), dst_ref=dst, send_sem=plane_s.at[stage, d], recv_sem=plane_r.at[stage, d],
                device_id=(zi * nplane + q, rep), device_id_type=MESH)))
        return copies

    def arrive(copies):
        for copy in copies:
            copy.wait_recv()

    def place(grp):
        z, x, y = grp // nplane, grp % nplane // ny, grp % ny
        return (x + z) % nx * block + z * (ny * 4) + y * 4

    def member(c, u):
        v = (u * 5 + zi * ny + pi % ny) % (nz * ny)
        z, y = v // ny, v % ny
        return z * nplane + (c + nx * nz - z) % nx * ny + y, z, y

    def to_owner(stage, src, dst, grp):
        return pltpu.make_async_remote_copy(
            src_ref=src, dst_ref=dst, send_sem=all_s.at[stage], recv_sem=all_r.at[stage],
            device_id=(grp, rep), device_id_type=MESH)

    loads[0].wait()
    uhigh, ulow = split(ufac[...].T)
    core_copies = []
    for c in range(nx):
        loads[2 + c].wait()
        lo = c * width
        total = jnp.zeros((rank, width), F32)
        for k in range(0, rows, depth):
            high, low = split(snap[k:k + depth, lo:lo + width])
            shigh[k:k + depth, lo:lo + width] = high
            slow[k:k + depth, lo:lo + width] = low
            uh, ul = uhigh[:, k:k + depth], ulow[:, k:k + depth]
            total = total + (half(uh, high) + (half(ul, high) + half(uh, low)))
        for core in range(2):
            for z in range(nz):
                for k in range(tiles):
                    at = c * block + z * ny * 4 + k * 8
                    proj[core, at:at + 8, :] = total[core * rhalf + z * 8:core * rhalf + z * 8 + 8, k * 128:k * 128 + 128]
        cut = pl.ds(c * block, block)
        core_copies.append(to_core(c, proj.at[sibling, cut], other.at[cut]))

    pl.semaphore_wait(word_sem, nz - 1)

    for c in range(nx):
        arrive(core_copies[c])
        at = c * block
        piece[at:at + block, :] = proj[rep, at:at + block, :] + other[at:at + block, :]

        def send(u, carry):
            grp, z, y = member(c, u)

            @pl.when(grp != me)
            def _():
                to_owner(0, piece.at[pl.ds(at + z * (ny * 4) + y * 4, 4)], owned.at[pl.ds(me * 4, 4)], grp).start()

            return carry

        lax.fori_loop(0, nz * ny, send, 0)
    pltpu.make_async_copy(piece.at[pl.ds(place(me), 4)], owned.at[pl.ds(me * 4, 4)], all_r.at[0]).start()
    pltpu.make_async_copy(owned, owned, all_r.at[0]).wait()
    flat = jnp.concatenate([owned[pl.ds(c, count, stride=4), :] for c in range(4)], axis=1)

    loads[1].wait()
    tpart[...] = full(full(tfac[...], flat), flat, NT)
    thalf = tpart.shape[0] // 2
    tmine = pl.ds(rep * thalf, thalf)
    arrive(to_core(nx, tpart.at[pl.ds(sibling * thalf, thalf)], tother))
    tchip[...] = tpart[tmine, :] + tother[...]
    keeper = (pi // ny + zi) % ny == pi % ny
    my_row = zi * nx + pi // ny

    def send_row(u, carry):
        j = (u * 5 + zi * ny + pi % ny) % (nz * nx)
        z, x = j // nx, j % nx
        grp = z * nplane + x * ny + (x + z) % ny

        @pl.when(grp != me)
        def _():
            to_owner(2, tchip.at[pl.ds(j, 1)], trows.at[pl.ds(me, 1)], grp).start()

        return carry

    lax.fori_loop(0, nz * nx, send_row, 0)
    spot = pl.ds(rep * thalf + my_row, 1)

    @pl.when(keeper)
    def _():
        pltpu.make_async_copy(tchip.at[pl.ds(my_row, 1)], trows.at[pl.ds(me, 1)], all_r.at[2]).start()
        pltpu.make_async_copy(trows, trows, all_r.at[2]).wait()
        tsum[...] = jnp.sum(trows[...], axis=0, keepdims=True)
        for c in range(nx):
            def send_sum(u, carry):
                grp, _, _ = member(c, u)

                @pl.when(grp != me)
                def _():
                    to_owner(3, tsum, tall.at[spot], grp).start()

                return carry

            lax.fori_loop(0, nz * ny, send_sum, 0)
        pltpu.make_async_copy(tsum, tall.at[spot], all_r.at[3]).start()

    pltpu.make_async_copy(tchip, tchip, all_r.at[3]).wait()
    arrive(to_core(nx + 1, tall.at[tmine], tall.at[tmine]))
    start = tall[...]

    scale = 1.0 / jnp.sqrt(jnp.sum(start * start, axis=(0, 1), keepdims=True) + 1e-06)

    def time_step(_, basis):
        return 1.5 * basis - 0.5 * full(full(basis, basis, NT), basis)

    basis = lax.fori_loop(0, STEPS, time_step, start * scale)
    time_out[...] = basis * math.sqrt(count)
    mixed = full(full(basis.T, basis), flat)
    for c in range(4):
        wback[pl.ds(c, count, stride=4), :] = mixed[:, c * 128:(c + 1) * 128]

    spot = pl.ds(place(me), 4)

    for c in range(nx):
        def send_back(u, carry):
            grp, _, _ = member(c, u)

            @pl.when(grp != me)
            def _():
                to_owner(1, wback.at[pl.ds(grp * 4, 4)], wpieces.at[rep, spot], grp).start()

            return carry

        lax.fori_loop(0, nz * ny, send_back, 0)
    pltpu.make_async_copy(wback.at[pl.ds(me * 4, 4)], wpieces.at[rep, spot], all_r.at[1]).start()
    pltpu.make_async_copy(wback, wback, all_r.at[1]).wait()
    arrive(to_core(nx + 2, wpieces.at[rep], wpieces.at[rep]))
    for core in range(2):
        for m in range(nz // 2):
            for c in range(nx):
                for k in range(tiles):
                    at = c * block + 2 * m * ny * 4 + k * 8
                    both = jnp.concatenate(
                        [wpieces[core, at:at + 8, :], wpieces[core, at + ny * 4:at + ny * 4 + 8, :]], axis=0)
                    high, low = split(both)
                    row, lo = core * rhalf + m * 16, c * width + k * 128
                    whigh[row:row + 16, lo:lo + 128] = high
                    wlow[row:row + 16, lo:lo + 128] = low

    part = rows // PARTS
    prows = part // nplane
    summed, crossed, spread = [], [], []
    for h in range(PARTS):
        for k in range(h * part, (h + 1) * part, min(part, 256)):
            high, low = shigh[k:k + min(part, 256), :], slow[k:k + min(part, 256), :]
            prod[k:k + min(part, 256), :] = half(high, whigh[...], NT) + (
                half(high, wlow[...], NT) + half(low, whigh[...], NT))
        summed.append(in_plane(h, lambda q: prod.at[pl.ds(h * part + q * prows, prows)], pin.at[h, pi]))
        pin[h, pi] = prod[pl.ds(h * part + pi * prows, prows), :]
    for h in range(PARTS):
        arrive(summed[h])
        psum[h] = functools.reduce(jnp.add, [pin[h, k] for k in range(nplane)])
        crossed.append(along_z(h, psum.at[h], pz.at[h, zi]))
        pz[h, zi] = psum[h]
    for h in range(PARTS):
        arrive(crossed[h])
        mine = pl.ds(h * part + pi * prows, prows)
        xall[mine, :] = functools.reduce(jnp.add, [pz[h, k] for k in range(nz)])
        spread.append(in_plane(PARTS + h, lambda q: xall.at[mine], xall.at[mine]))
    gram = jnp.zeros((rank, rank), F32)
    for h in range(PARTS):
        arrive(spread[h])
        some = xall[h * part:(h + 1) * part, :]
        gram = gram + full(some.T, some)
    gpart[...] = gram
    arrive(to_core(nx + 3, gpart, gother))
    gram = gpart[...] + gother[...]

    eye = jnp.where(
        lax.broadcasted_iota(jnp.int32, gram.shape, 0) == lax.broadcasted_iota(jnp.int32, gram.shape, 1), 1.0, 0.0
    ).astype(F32)
    norm = 1.0 / (jnp.sum(gram * eye, axis=(0, 1), keepdims=True) + 1e-06)
    inner, power = gram * norm, eye
    for _ in range(STEPS - 1):
        factor = 1.5 * eye - 0.5 * inner
        inner, power = full(factor, full(factor, inner)), full(factor, power)
    power = full(power, 1.5 * eye - 0.5 * inner)
    rows_out[...] = full(xall[...], power * (math.sqrt(2 * rows) * jnp.sqrt(norm)))
    for copy in started:
        copy.wait_send()
    rest = pl.ds(0, (count - 1) * 4)
    for stage in range(2):
        pltpu.make_async_copy(owned.at[rest], owned.at[rest], all_s.at[stage]).wait()

    @pl.when(keeper)
    def _():
        less, sent = pl.ds(0, nz * nx - 1), pl.ds(0, count - 1)
        pltpu.make_async_copy(tchip.at[less], tchip.at[less], all_s.at[2]).wait()
        pltpu.make_async_copy(trows.at[sent], trows.at[sent], all_s.at[3]).wait()

    @pl.when(jnp.logical_not(keeper))
    def _():
        pltpu.make_async_copy(tchip, tchip, all_s.at[2]).wait()


def solution(mesh):
    nz, nx, ny = dims = DIMS
    nplane = nx * ny
    count = nz * nplane

    def on_device(snapshots, row_factor, time_factor):
        _, rows, cols = snapshots.shape
        rank = row_factor.shape[1]
        modes = time_factor.shape[1]
        vmem = lambda *shape: pltpu.VMEM(shape, F32)
        narrow = lambda *shape: pltpu.VMEM(shape, BF16)
        sems = lambda *shape: pltpu.SemaphoreType.DMA(shape)
        part = rows // PARTS
        prows = part // nplane
        new_rows, new_time = pl.pallas_call(
            functools.partial(kernel, dims),
            out_shape=(
                jax.ShapeDtypeStruct((rows, rank), F32),
                jax.ShapeDtypeStruct((modes, count), F32),
            ),
            in_specs=[pl.BlockSpec(memory_space=pltpu.HBM)] * 3,
            out_specs=(pl.BlockSpec(memory_space=pltpu.VMEM),) * 2,
            scratch_shapes=[
                vmem(rows, cols), vmem(rows, rank), vmem(modes, count), narrow(rows, cols), narrow(rows, cols),
                vmem(2, count * 4, 128), vmem(count * 4, 128), vmem(count * 4, 128), vmem(count * 4, 128),
                vmem(modes, count), vmem(modes // 2, count), vmem(modes // 2, count),
                vmem(count, count), vmem(1, count), vmem(modes, count),
                vmem(count * 4, 128), vmem(2, count * 4, 128),
                narrow(rank, cols), narrow(rank, cols),
                vmem(rows, rank), vmem(PARTS, nplane, prows, rank), vmem(PARTS, prows, rank),
                vmem(PARTS, nz, prows, rank), vmem(rows, rank), vmem(rank, rank), vmem(rank, rank),
                sems(nx + 2), sems(nx + 4), sems(nx + 4), sems(2 * PARTS, nplane), sems(2 * PARTS, nplane),
                sems(PARTS, nz), sems(PARTS, nz), sems(4), sems(4), pltpu.SemaphoreType.REGULAR,
            ],
            compiler_params=pltpu.CompilerParams(
                collective_id=0, has_side_effects=True, vmem_limit_bytes=VMEM_MIB * 1024 * 1024),
        )(*(pltpu.with_memory_space_constraint(arg, pltpu.HBM) for arg in (snapshots, row_factor, time_factor.T)))
        return new_rows, new_time.T

    return jax.shard_map(
        on_device,
        mesh=mesh,
        in_specs=(P("grp", "rep", None), P("rep", None), P()),
        out_specs=(P("rep", None), P()),
        check_vma=False,
    )
```

```python
import functools
import math

import jax
import jax.numpy as jnp
from jax import lax
from jax.experimental import pallas as pl
from jax.experimental.pallas import tpu as pltpu
from jax.sharding import PartitionSpec as P

MESH = pl.DeviceIdType.MESH
STEPS = 8
DIMS = (8, 4, 4)
PARTS = 4
VMEM_MIB = 40
F32 = jnp.float32
BF16 = jnp.bfloat16
NN = (((1,), (0,)), ((), ()))
NT = (((1,), (1,)), ((), ()))


def full(left, right, dims=NN):
    return lax.dot_general(left, right, dims, precision=lax.Precision.HIGHEST, preferred_element_type=F32)


def half(left, right, dims=NN):
    return lax.dot_general(left, right, dims, preferred_element_type=F32)


def split(value):
    high = value.astype(BF16)
    return high, (value - high.astype(F32)).astype(BF16)


def far(size):
    return sorted(range(size), key=lambda d: -min(d, size - d))


def kernel(dims, snap_ref, row_ref, time_ref, rows_out, time_out,
           snap, ufac, tfac, shigh, slow, proj, other, piece, owned,
           tpart, tz, tsum, tplane, tall,
           wback, wpieces, whigh, wlow,
           prod, pin, psum, pz, xall, gpart, gother,
           load_sem, core_s, core_r, plane_s, plane_r, z_s, z_r, all_s, all_r, word_sem):
    nz, nx, ny = dims
    nplane = nx * ny
    count = nz * nplane
    me = lax.axis_index("grp")
    rep = lax.axis_index("rep")
    zi, pi = me // nplane, me % nplane
    sibling = 1 - rep
    rank = ufac.shape[1]
    rhalf = rank // 2
    rows, cols = snap.shape
    tiles = ny // 2
    width = tiles * 128
    block = nz * ny * 4
    depth = min(rows, 256)

    loads = [pltpu.make_async_copy(row_ref, ufac, load_sem.at[nx]), pltpu.make_async_copy(time_ref, tfac, load_sem.at[nx + 1])]
    for c in range(nx):
        cut = pl.ds(c * width, width)
        loads.append(pltpu.make_async_copy(snap_ref.at[0, :, cut], snap.at[:, cut], load_sem.at[c]))
    for load in loads:
        load.start()

    barrier = pltpu.get_barrier_semaphore()

    def greet(grp, core):
        pl.semaphore_signal(barrier, inc=1, device_id=(grp, core), device_id_type=MESH)

    greet(me, sibling)
    for d in range(1, nz):
        greet((zi + d) % nz * nplane + pi, rep)
    for d in range(1, nplane):
        greet(zi * nplane + (pi + d) % nplane, rep)
    pl.semaphore_wait(barrier, nz + nplane - 1)
    for d in range(1, nz):
        pl.semaphore_signal(
            word_sem, inc=1, device_id=((zi + d) % nz * nplane + pi, rep), device_id_type=MESH)
    pl.semaphore_signal(word_sem, inc=1, device_id=(me, sibling), device_id_type=MESH)

    started = []

    def begin(copy):
        copy.start()
        started.append(copy)
        return copy

    def to_core(stage, src, dst):
        return [begin(pltpu.make_async_remote_copy(
            src_ref=src, dst_ref=dst, send_sem=core_s.at[stage], recv_sem=core_r.at[stage],
            device_id=(me, sibling), device_id_type=MESH))]

    def along_z(stage, src, dst):
        return [begin(pltpu.make_async_remote_copy(
            src_ref=src((zi + d) % nz), dst_ref=dst, send_sem=z_s.at[stage, d], recv_sem=z_r.at[stage, d],
            device_id=((zi + d) % nz * nplane + pi, rep), device_id_type=MESH)) for d in range(1, nz)]

    def in_plane(stage, src, dst):
        copies = []
        for d in range(1, nplane):
            q = (pi + d) % nplane
            copies.append(begin(pltpu.make_async_remote_copy(
                src_ref=src(q), dst_ref=dst, send_sem=plane_s.at[stage, d], recv_sem=plane_r.at[stage, d],
                device_id=(zi * nplane + q, rep), device_id_type=MESH)))
        return copies

    def arrive(copies):
        for copy in copies:
            copy.wait_recv()

    def place(grp):
        z, x, y = grp // nplane, grp % nplane // ny, grp % ny
        return (x + z) % nx * block + z * (ny * 4) + y * 4

    def to_owner(stage, src, dst, grp, landed=0):
        return pltpu.make_async_remote_copy(
            src_ref=src, dst_ref=dst, send_sem=all_s.at[stage], recv_sem=all_r.at[landed],
            device_id=(grp, rep), device_id_type=MESH)

    zs = [(zi + d) % nz for d in far(nz)]
    xs = [(pi // ny + d) % nx for d in far(nx)]
    ys = [(pi % ny + d) % ny for d in far(ny)]

    loads[0].wait()
    uhigh, ulow = split(ufac[...].T)
    core_copies = []
    for c in range(nx):
        loads[2 + c].wait()
        lo = c * width
        total = jnp.zeros((rank, width), F32)
        for k in range(0, rows, depth):
            high, low = split(snap[k:k + depth, lo:lo + width])
            shigh[k:k + depth, lo:lo + width] = high
            slow[k:k + depth, lo:lo + width] = low
            uh, ul = uhigh[:, k:k + depth], ulow[:, k:k + depth]
            total = total + (half(uh, high) + (half(ul, high) + half(uh, low)))
        for core in range(2):
            for z in range(nz):
                for k in range(tiles):
                    at = c * block + z * ny * 4 + k * 8
                    proj[core, at:at + 8, :] = total[core * rhalf + z * 8:core * rhalf + z * 8 + 8, k * 128:k * 128 + 128]
        cut = pl.ds(c * block, block)
        core_copies.append(to_core(c, proj.at[sibling, cut], other.at[cut]))

    pl.semaphore_wait(word_sem, nz)

    for c in range(nx):
        arrive(core_copies[c])
        at = c * block
        piece[at:at + block, :] = proj[rep, at:at + block, :] + other[at:at + block, :]

        for z in zs:
            for y in ys:
                x = (c + nx * nz - z) % nx
                copy = to_owner(
                    0, piece.at[pl.ds(at + z * (ny * 4) + y * 4, 4)], owned.at[pl.ds(me * 4, 4)], z * nplane + x * ny + y)
                if z is zs[-1] and y is ys[-1]:
                    pl.when(x != pi // ny)(copy.start)
                else:
                    copy.start()
    pltpu.make_async_copy(piece.at[pl.ds(place(me), 4)], owned.at[pl.ds(me * 4, 4)], all_r.at[0]).start()
    pltpu.make_async_copy(owned, owned, all_r.at[0]).wait()
    flat = jnp.concatenate([owned[pl.ds(c, count, stride=4), :] for c in range(4)], axis=1)

    loads[1].wait()
    tpart[...] = full(full(tfac[...], flat), flat, NT)
    trows = tpart.shape[0] // nz
    copies = along_z(PARTS, lambda q: tpart.at[pl.ds(q * trows, trows)], tz.at[zi])
    tz[zi] = tpart[pl.ds(zi * trows, trows), :]
    arrive(copies)
    tsum[...] = functools.reduce(jnp.add, [tz[k] for k in range(nz)])
    copies = in_plane(2 * PARTS, lambda q: tsum, tplane.at[rep, pi])
    for d in range(nplane):
        copies.append(begin(pltpu.make_async_remote_copy(
            src_ref=tsum, dst_ref=tplane.at[rep, pi], send_sem=plane_s.at[2 * PARTS + 1, d],
            recv_sem=plane_r.at[2 * PARTS + 1, d], device_id=(zi * nplane + (pi + d) % nplane, sibling),
            device_id_type=MESH)))
    tplane[rep, pi] = tsum[...]
    arrive(copies)
    tmine = pl.ds(zi * trows, trows)
    tall[tmine, :] = functools.reduce(jnp.add, [tplane[core, k] for core in range(2) for k in range(nplane)])
    arrive(along_z(PARTS + 1, lambda q: tall.at[tmine], tall.at[tmine]))
    start = tall[...]

    scale = 1.0 / jnp.sqrt(jnp.sum(start * start, axis=(0, 1), keepdims=True) + 1e-06)

    basis = start * scale
    for _ in range(STEPS):
        basis = 1.5 * basis - 0.5 * full(full(basis, basis, NT), basis)
    time_out[...] = basis * math.sqrt(count)
    mixed = full(full(basis.T, basis), flat)
    for c in range(4):
        wback[pl.ds(c, count, stride=4), :] = mixed[:, c * 128:(c + 1) * 128]

    spot = pl.ds(place(me), 4)

    my_part = (pi // ny + zi) % nx
    for z in zs:
        for x in xs:
            for y in ys:
                if not (z is zs[-1] and x is xs[-1] and y is ys[-1]):
                    grp = z * nplane + x * ny + y
                    to_owner(1, wback.at[pl.ds(grp * 4, 4)], wpieces.at[rep, spot], grp, 1 + my_part).start()
    pltpu.make_async_copy(wback.at[pl.ds(me * 4, 4)], wpieces.at[rep, spot], all_r.at[1 + my_part]).start()
    passed = []
    for c in range(nx):
        cut = pl.ds(c * block, block)
        pltpu.make_async_copy(wback.at[cut], wpieces.at[rep, cut], all_r.at[1 + c]).wait()
        passed.append(to_core(nx + c, wpieces.at[rep, cut], wpieces.at[rep, cut]))

    def narrowed(core, c):
        for m in range(nz // 2):
            for k in range(tiles):
                at = c * block + 2 * m * ny * 4 + k * 8
                both = jnp.concatenate(
                    [wpieces[core, at:at + 8, :], wpieces[core, at + ny * 4:at + ny * 4 + 8, :]], axis=0)
                high, low = split(both)
                row, lo = pl.ds(pl.multiple_of(core * rhalf + m * 16, 16), 16), c * width + k * 128
                whigh[row, lo:lo + 128] = high
                wlow[row, lo:lo + 128] = low

    for c in range(nx):
        narrowed(rep, c)
    for c in range(nx):
        arrive(passed[c])
        narrowed(sibling, c)

    part = rows // PARTS
    prows = part // nplane
    summed, crossed, spread = [], [], []
    for h in range(PARTS):
        for k in range(h * part, (h + 1) * part, min(part, 256)):
            high, low = shigh[k:k + min(part, 256), :], slow[k:k + min(part, 256), :]
            prod[k:k + min(part, 256), :] = half(high, whigh[...], NT) + (
                half(high, wlow[...], NT) + half(low, whigh[...], NT))
        summed.append(in_plane(h, lambda q: prod.at[pl.ds(h * part + q * prows, prows)], pin.at[h, pi]))
        pin[h, pi] = prod[pl.ds(h * part + pi * prows, prows), :]
    for h in range(PARTS):
        arrive(summed[h])
        psum[h] = functools.reduce(jnp.add, [pin[h, k] for k in range(nplane)])
        crossed.append(along_z(h, lambda q: psum.at[h], pz.at[h, zi]))
        pz[h, zi] = psum[h]
    for h in range(PARTS):
        arrive(crossed[h])
        mine = pl.ds(h * part + pi * prows, prows)
        xall[mine, :] = functools.reduce(jnp.add, [pz[h, k] for k in range(nz)])
        spread.append(in_plane(PARTS + h, lambda q: xall.at[mine], xall.at[mine]))
    gram = jnp.zeros((rank, rank), F32)
    for h in range(PARTS):
        arrive(spread[h])
        some = xall[h * part:(h + 1) * part, :]
        gram = gram + full(some.T, some)
    gpart[...] = gram
    arrive(to_core(2 * nx, gpart, gother))
    gram = gpart[...] + gother[...]

    eye = jnp.where(
        lax.broadcasted_iota(jnp.int32, gram.shape, 0) == lax.broadcasted_iota(jnp.int32, gram.shape, 1), 1.0, 0.0
    ).astype(F32)
    norm = 1.0 / (jnp.sum(gram * eye, axis=(0, 1), keepdims=True) + 1e-06)
    inner, power = gram * norm, eye
    for _ in range(STEPS - 1):
        factor = 1.5 * eye - 0.5 * inner
        inner, power = full(factor, full(factor, inner)), full(factor, power)
    power = full(power, 1.5 * eye - 0.5 * inner)
    rows_out[...] = full(xall[...], power * (math.sqrt(2 * rows) * jnp.sqrt(norm)))
    for copy in started:
        copy.wait_send()
    rest = pl.ds(0, (count - 1) * 4)
    for stage in range(2):
        pltpu.make_async_copy(owned.at[rest], owned.at[rest], all_s.at[stage]).wait()


def solution(mesh):
    nz, nx, ny = dims = DIMS
    nplane = nx * ny
    count = nz * nplane

    def on_device(snapshots, row_factor, time_factor):
        _, rows, cols = snapshots.shape
        rank = row_factor.shape[1]
        modes = time_factor.shape[1]
        vmem = lambda *shape: pltpu.VMEM(shape, F32)
        narrow = lambda *shape: pltpu.VMEM(shape, BF16)
        sems = lambda *shape: pltpu.SemaphoreType.DMA(shape)
        part = rows // PARTS
        prows = part // nplane
        new_rows, new_time = pl.pallas_call(
            functools.partial(kernel, dims),
            out_shape=(
                jax.ShapeDtypeStruct((rows, rank), F32),
                jax.ShapeDtypeStruct((modes, count), F32),
            ),
            in_specs=[pl.BlockSpec(memory_space=pltpu.HBM)] * 3,
            out_specs=(pl.BlockSpec(memory_space=pltpu.VMEM),) * 2,
            scratch_shapes=[
                vmem(rows, cols), vmem(rows, rank), vmem(modes, count), narrow(rows, cols), narrow(rows, cols),
                vmem(2, count * 4, 128), vmem(count * 4, 128), vmem(count * 4, 128), vmem(count * 4, 128),
                vmem(modes, count), vmem(nz, modes // nz, count), vmem(modes // nz, count),
                vmem(2, nplane, modes // nz, count), vmem(modes, count),
                vmem(count * 4, 128), vmem(2, count * 4, 128),
                narrow(rank, cols), narrow(rank, cols),
                vmem(rows, rank), vmem(PARTS, nplane, prows, rank), vmem(PARTS, prows, rank),
                vmem(PARTS, nz, prows, rank), vmem(rows, rank), vmem(rank, rank), vmem(rank, rank),
                sems(nx + 2), sems(2 * nx + 1), sems(2 * nx + 1), sems(2 * PARTS + 2, nplane), sems(2 * PARTS + 2, nplane),
                sems(PARTS + 2, nz), sems(PARTS + 2, nz), sems(2), sems(1 + nx), pltpu.SemaphoreType.REGULAR,
            ],
            compiler_params=pltpu.CompilerParams(
                collective_id=0, has_side_effects=True, vmem_limit_bytes=VMEM_MIB * 1024 * 1024),
        )(*(pltpu.with_memory_space_constraint(arg, pltpu.HBM) for arg in (snapshots, row_factor, time_factor.T)))
        return new_rows, new_time.T

    return jax.shard_map(
        on_device,
        mesh=mesh,
        in_specs=(P("grp", "rep", None), P("rep", None), P()),
        out_specs=(P("rep", None), P()),
        check_vma=False,
    )
```

```python
import functools
import math

import jax
import jax.numpy as jnp
from jax import lax
from jax.experimental import pallas as pl
from jax.experimental.pallas import tpu as pltpu
from jax.sharding import PartitionSpec as P

MESH = pl.DeviceIdType.MESH
STEPS = 8
DIMS = (8, 4, 4)
PARTS = 4
VMEM_MIB = 40
F32 = jnp.float32
BF16 = jnp.bfloat16
NN = (((1,), (0,)), ((), ()))
NT = (((1,), (1,)), ((), ()))


def full(left, right, dims=NN):
    return lax.dot_general(left, right, dims, precision=lax.Precision.HIGHEST, preferred_element_type=F32)


def half(left, right, dims=NN):
    return lax.dot_general(left, right, dims, preferred_element_type=F32)


def split(value):
    high = value.astype(BF16)
    return high, (value - high.astype(F32)).astype(BF16)


def far(size):
    return sorted(range(size), key=lambda d: -min(d, size - d))


def kernel(dims, snap_ref, row_ref, time_ref, rows_out, time_out,
           snap, ufac, tfac, shigh, slow, proj, other, piece, owned,
           tpart, tz, tsum, tplane, tall,
           wback, wpieces, wcut,
           prod, pin, psum, pz, xall, gpart, gother,
           load_sem, core_s, core_r, plane_s, plane_r, z_s, z_r, all_s, all_r, word_sem):
    nz, nx, ny = dims
    nplane = nx * ny
    count = nz * nplane
    me = lax.axis_index("grp")
    rep = lax.axis_index("rep")
    zi, pi = me // nplane, me % nplane
    sibling = 1 - rep
    rank = ufac.shape[1]
    rhalf = rank // 2
    rows, cols = snap.shape
    tiles = ny // 2
    width = tiles * 128
    block = nz * ny * 4
    depth = min(rows, 256)

    loads = [pltpu.make_async_copy(row_ref, ufac, load_sem.at[nx]), pltpu.make_async_copy(time_ref, tfac, load_sem.at[nx + 1])]
    for c in range(nx):
        cut = pl.ds(c * width, width)
        loads.append(pltpu.make_async_copy(snap_ref.at[0, :, cut], snap.at[:, cut], load_sem.at[c]))
    for load in loads:
        load.start()

    barrier = pltpu.get_barrier_semaphore()

    def greet(grp, core):
        pl.semaphore_signal(barrier, inc=1, device_id=(grp, core), device_id_type=MESH)

    greet(me, sibling)
    for d in range(1, nz):
        greet((zi + d) % nz * nplane + pi, rep)
    for d in range(1, nplane):
        greet(zi * nplane + (pi + d) % nplane, rep)
    pl.semaphore_wait(barrier, nz + nplane - 1)
    for d in range(1, nz):
        pl.semaphore_signal(
            word_sem, inc=1, device_id=((zi + d) % nz * nplane + pi, rep), device_id_type=MESH)
    pl.semaphore_signal(word_sem, inc=1, device_id=(me, sibling), device_id_type=MESH)

    ring = sorted(
        ((dx, dy) for dx in range(nx) for dy in range(ny)),
        key=lambda at: -min(at[0], nx - at[0]) - min(at[1], ny - at[1]))
    started = []

    def begin(copy):
        copy.start()
        started.append(copy)
        return copy

    def to_core(stage, src, dst):
        return [begin(pltpu.make_async_remote_copy(
            src_ref=src, dst_ref=dst, send_sem=core_s.at[stage], recv_sem=core_r.at[stage],
            device_id=(me, sibling), device_id_type=MESH))]

    def along_z(stage, src, dst):
        return [begin(pltpu.make_async_remote_copy(
            src_ref=src((zi + d) % nz), dst_ref=dst, send_sem=z_s.at[stage, d], recv_sem=z_r.at[stage, d],
            device_id=((zi + d) % nz * nplane + pi, rep), device_id_type=MESH)) for d in far(nz)[:-1]]

    def in_plane(stage, src, dst):
        copies = []
        for dx, dy in ring[:-1]:
            q = (pi // ny + dx) % nx * ny + (pi % ny + dy) % ny
            copies.append(begin(pltpu.make_async_remote_copy(
                src_ref=src(q), dst_ref=dst, send_sem=plane_s.at[stage, dx * ny + dy],
                recv_sem=plane_r.at[stage, dx * ny + dy],
                device_id=(zi * nplane + q, rep), device_id_type=MESH)))
        return copies

    def arrive(copies):
        for copy in copies:
            copy.wait_recv()

    def place(grp):
        z, x, y = grp // nplane, grp % nplane // ny, grp % ny
        return (x + z) % nx * block + z * (ny * 4) + y * 4

    def to_owner(stage, src, dst, grp, landed=0):
        return pltpu.make_async_remote_copy(
            src_ref=src, dst_ref=dst, send_sem=all_s.at[stage], recv_sem=all_r.at[landed],
            device_id=(grp, rep), device_id_type=MESH)

    zs = [(zi + d) % nz for d in far(nz)]
    xs = [(pi // ny + d) % nx for d in far(nx)]
    ys = [(pi % ny + d) % ny for d in far(ny)]

    loads[0].wait()
    ucut = jnp.concatenate(split(ufac[...].T), axis=0)
    core_copies = []
    for c in range(nx):
        loads[2 + c].wait()
        lo = c * width
        total = jnp.zeros((rank, width), F32)
        for k in range(0, rows, depth):
            high, low = split(snap[k:k + depth, lo:lo + width])
            shigh[k:k + depth, lo:lo + width] = high
            slow[k:k + depth, lo:lo + width] = low
            first = half(ucut[:, k:k + depth], high)
            total = total + (first[:rank] + (first[rank:] + half(ucut[:rank, k:k + depth], low)))
        for core in range(2):
            for z in range(nz):
                for k in range(tiles):
                    at = c * block + z * ny * 4 + k * 8
                    proj[core, at:at + 8, :] = total[core * rhalf + z * 8:core * rhalf + z * 8 + 8, k * 128:k * 128 + 128]
        cut = pl.ds(c * block, block)
        core_copies.append(to_core(c, proj.at[sibling, cut], other.at[cut]))

    pl.semaphore_wait(word_sem, nz)

    for c in range(nx):
        arrive(core_copies[c])
        at = c * block
        piece[at:at + block, :] = proj[rep, at:at + block, :] + other[at:at + block, :]

        for z in zs:
            for y in ys:
                x = (c + nx * nz - z) % nx
                copy = to_owner(
                    0, piece.at[pl.ds(at + z * (ny * 4) + y * 4, 4)], owned.at[pl.ds(me * 4, 4)], z * nplane + x * ny + y)
                if z is zs[-1] and y is ys[-1]:
                    pl.when(x != pi // ny)(copy.start)
                else:
                    copy.start()
    pltpu.make_async_copy(piece.at[pl.ds(place(me), 4)], owned.at[pl.ds(me * 4, 4)], all_r.at[0]).start()
    pltpu.make_async_copy(owned, owned, all_r.at[0]).wait()
    flat = jnp.concatenate([owned[pl.ds(c, count, stride=4), :] for c in range(4)], axis=1)

    loads[1].wait()
    tpart[...] = full(full(tfac[...], flat), flat, NT)
    trows = tpart.shape[0] // nz
    copies = along_z(PARTS, lambda q: tpart.at[pl.ds(q * trows, trows)], tz.at[zi])
    tz[zi] = tpart[pl.ds(zi * trows, trows), :]
    arrive(copies)
    tsum[...] = functools.reduce(jnp.add, [tz[k] for k in range(nz)])
    copies = in_plane(2 * PARTS, lambda q: tsum, tplane.at[rep, pi])
    for dx, dy in ring:
        q = (pi // ny + dx) % nx * ny + (pi % ny + dy) % ny
        copies.append(begin(pltpu.make_async_remote_copy(
            src_ref=tsum, dst_ref=tplane.at[rep, pi], send_sem=plane_s.at[2 * PARTS + 1, dx * ny + dy],
            recv_sem=plane_r.at[2 * PARTS + 1, dx * ny + dy], device_id=(zi * nplane + q, sibling),
            device_id_type=MESH)))
    tplane[rep, pi] = tsum[...]
    arrive(copies)
    tmine = pl.ds(zi * trows, trows)
    tall[tmine, :] = functools.reduce(jnp.add, [tplane[core, k] for core in range(2) for k in range(nplane)])
    arrive(along_z(PARTS + 1, lambda q: tall.at[tmine], tall.at[tmine]))
    start = tall[...]

    scale = 1.0 / jnp.sqrt(jnp.sum(start * start, axis=(0, 1), keepdims=True) + 1e-06)

    basis = start * scale
    for _ in range(STEPS):
        basis = 1.5 * basis - 0.5 * full(full(basis, basis, NT), basis)
    time_out[...] = basis * math.sqrt(count)
    mixed = full(full(basis.T, basis), flat)
    for c in range(4):
        wback[pl.ds(c, count, stride=4), :] = mixed[:, c * 128:(c + 1) * 128]

    spot = pl.ds(place(me), 4)

    my_part = (pi // ny + zi) % nx
    for z in zs:
        for x in xs:
            for y in ys:
                if not (z is zs[-1] and x is xs[-1] and y is ys[-1]):
                    grp = z * nplane + x * ny + y
                    to_owner(1, wback.at[pl.ds(grp * 4, 4)], wpieces.at[rep, spot], grp, 1 + my_part).start()
    pltpu.make_async_copy(wback.at[pl.ds(me * 4, 4)], wpieces.at[rep, spot], all_r.at[1 + my_part]).start()
    passed = []
    for c in range(nx):
        cut = pl.ds(c * block, block)
        pltpu.make_async_copy(wback.at[cut], wpieces.at[rep, cut], all_r.at[1 + c]).wait()
        passed.append(to_core(nx + c, wpieces.at[rep, cut], wpieces.at[rep, cut]))

    def narrowed(core, c):
        for m in range(nz // 2):
            for k in range(tiles):
                at = c * block + 2 * m * ny * 4 + k * 8
                both = jnp.concatenate(
                    [wpieces[core, at:at + 8, :], wpieces[core, at + ny * 4:at + ny * 4 + 8, :]], axis=0)
                high, low = split(both)
                row, lo = pl.ds(pl.multiple_of(core * rhalf + m * 16, 16), 16), c * width + k * 128
                wcut[row, lo:lo + 128] = high
                wcut[pl.ds(pl.multiple_of(rank + core * rhalf + m * 16, 16), 16), lo:lo + 128] = low

    for c in range(nx):
        narrowed(rep, c)
    for c in range(nx):
        arrive(passed[c])
        narrowed(sibling, c)

    part = rows // PARTS
    prows = part // nplane
    summed, crossed, spread = [], [], []
    for h in range(PARTS):
        for k in range(h * part, (h + 1) * part, min(part, 256)):
            high, low = shigh[k:k + min(part, 256), :], slow[k:k + min(part, 256), :]
            first = half(high, wcut[...], NT)
            prod[k:k + min(part, 256), :] = first[:, :rank] + (first[:, rank:] + half(low, wcut[:rank, :], NT))
        summed.append(in_plane(h, lambda q: prod.at[pl.ds(h * part + q * prows, prows)], pin.at[h, pi]))
        pin[h, pi] = prod[pl.ds(h * part + pi * prows, prows), :]
    for h in range(PARTS):
        arrive(summed[h])
        psum[h] = functools.reduce(jnp.add, [pin[h, k] for k in range(nplane)])
        crossed.append(along_z(h, lambda q: psum.at[h], pz.at[h, zi]))
        pz[h, zi] = psum[h]
    for h in range(PARTS):
        arrive(crossed[h])
        mine = pl.ds(h * part + pi * prows, prows)
        xall[mine, :] = functools.reduce(jnp.add, [pz[h, k] for k in range(nz)])
        spread.append(in_plane(PARTS + h, lambda q: xall.at[mine], xall.at[mine]))
    gram = jnp.zeros((rank, rank), F32)
    for h in range(PARTS):
        arrive(spread[h])
        some = xall[h * part:(h + 1) * part, :]
        gram = gram + full(some.T, some)
    gpart[...] = gram
    arrive(to_core(2 * nx, gpart, gother))
    gram = gpart[...] + gother[...]

    eye = jnp.where(
        lax.broadcasted_iota(jnp.int32, gram.shape, 0) == lax.broadcasted_iota(jnp.int32, gram.shape, 1), 1.0, 0.0
    ).astype(F32)
    norm = 1.0 / (jnp.sum(gram * eye, axis=(0, 1), keepdims=True) + 1e-06)
    inner, power = gram * norm, eye
    for _ in range(STEPS - 1):
        factor = 1.5 * eye - 0.5 * inner
        inner, power = full(factor, full(factor, inner)), full(factor, power)
    power = full(power, 1.5 * eye - 0.5 * inner)
    rows_out[...] = full(xall[...], power * (math.sqrt(2 * rows) * jnp.sqrt(norm)))
    for copy in started:
        copy.wait_send()
    rest = pl.ds(0, (count - 1) * 4)
    for stage in range(2):
        pltpu.make_async_copy(owned.at[rest], owned.at[rest], all_s.at[stage]).wait()


def solution(mesh):
    nz, nx, ny = dims = DIMS
    nplane = nx * ny
    count = nz * nplane

    def on_device(snapshots, row_factor, time_factor):
        _, rows, cols = snapshots.shape
        rank = row_factor.shape[1]
        modes = time_factor.shape[1]
        vmem = lambda *shape: pltpu.VMEM(shape, F32)
        narrow = lambda *shape: pltpu.VMEM(shape, BF16)
        sems = lambda *shape: pltpu.SemaphoreType.DMA(shape)
        part = rows // PARTS
        prows = part // nplane
        new_rows, new_time = pl.pallas_call(
            functools.partial(kernel, dims),
            out_shape=(
                jax.ShapeDtypeStruct((rows, rank), F32),
                jax.ShapeDtypeStruct((modes, count), F32),
            ),
            in_specs=[pl.BlockSpec(memory_space=pltpu.HBM)] * 3,
            out_specs=(pl.BlockSpec(memory_space=pltpu.VMEM),) * 2,
            scratch_shapes=[
                vmem(rows, cols), vmem(rows, rank), vmem(modes, count), narrow(rows, cols), narrow(rows, cols),
                vmem(2, count * 4, 128), vmem(count * 4, 128), vmem(count * 4, 128), vmem(count * 4, 128),
                vmem(modes, count), vmem(nz, modes // nz, count), vmem(modes // nz, count),
                vmem(2, nplane, modes // nz, count), vmem(modes, count),
                vmem(count * 4, 128), vmem(2, count * 4, 128),
                narrow(2 * rank, cols),
                vmem(rows, rank), vmem(PARTS, nplane, prows, rank), vmem(PARTS, prows, rank),
                vmem(PARTS, nz, prows, rank), vmem(rows, rank), vmem(rank, rank), vmem(rank, rank),
                sems(nx + 2), sems(2 * nx + 1), sems(2 * nx + 1), sems(2 * PARTS + 2, nplane), sems(2 * PARTS + 2, nplane),
                sems(PARTS + 2, nz), sems(PARTS + 2, nz), sems(2), sems(1 + nx), pltpu.SemaphoreType.REGULAR,
            ],
            compiler_params=pltpu.CompilerParams(
                collective_id=0, has_side_effects=True, vmem_limit_bytes=VMEM_MIB * 1024 * 1024),
        )(*(pltpu.with_memory_space_constraint(arg, pltpu.HBM) for arg in (snapshots, row_factor, time_factor.T)))
        return new_rows, new_time.T

    return jax.shard_map(
        on_device,
        mesh=mesh,
        in_specs=(P("grp", "rep", None), P("rep", None), P()),
        out_specs=(P("rep", None), P()),
        check_vma=False,
    )
```

```python
import functools
import math

import jax
import jax.numpy as jnp
from jax import lax
from jax.experimental import pallas as pl
from jax.experimental.pallas import tpu as pltpu
from jax.sharding import PartitionSpec as P

MESH = pl.DeviceIdType.MESH
STEPS = 8
DIMS = (8, 4, 4)
PARTS = 4
VMEM_MIB = 40
F32 = jnp.float32
BF16 = jnp.bfloat16
NN = (((1,), (0,)), ((), ()))
NT = (((1,), (1,)), ((), ()))


def full(left, right, dims=NN):
    return lax.dot_general(left, right, dims, precision=lax.Precision.HIGHEST, preferred_element_type=F32)


def half(left, right, dims=NN):
    return lax.dot_general(left, right, dims, preferred_element_type=F32)


def split(value):
    high = value.astype(BF16)
    return high, (value - high.astype(F32)).astype(BF16)


def thirds(value):
    high, rest = value.astype(BF16), value
    rest = rest - high.astype(F32)
    mid = rest.astype(BF16)
    return high, mid, (rest - mid.astype(F32)).astype(BF16)


def beside(*blocks):
    return jnp.concatenate(blocks, axis=1)


def above(*blocks):
    return jnp.concatenate(blocks, axis=0)


def six(left, right):
    high, mid, low = left
    rhigh, rmid, rlow = right
    n = rhigh.shape[1]
    four = half(beside(high, mid), above(beside(rhigh, rmid), beside(rmid, rhigh)))
    two = half(beside(high, low), above(rlow, rhigh))
    return four[:, :n] + (four[:, n:] + two)


def far(size):
    return sorted(range(size), key=lambda d: -min(d, size - d))


def kernel(dims, snap_ref, row_ref, time_ref, rows_out, time_out,
           snap, ufac, tfac, shigh, slow, proj, other, piece, owned,
           tpart, tz, tsum, tplane, tall,
           wback, wpieces, wcut,
           prod, pin, psum, pz, xall, gpart, gother,
           load_sem, core_s, core_r, plane_s, plane_r, z_s, z_r, all_s, all_r, word_sem):
    nz, nx, ny = dims
    nplane = nx * ny
    count = nz * nplane
    me = lax.axis_index("grp")
    rep = lax.axis_index("rep")
    zi, pi = me // nplane, me % nplane
    sibling = 1 - rep
    rank = ufac.shape[1]
    rhalf = rank // 2
    rows, cols = snap.shape
    tiles = ny // 2
    width = tiles * 128
    block = nz * ny * 4
    depth = min(rows, 256)

    loads = [pltpu.make_async_copy(row_ref, ufac, load_sem.at[nx]), pltpu.make_async_copy(time_ref, tfac, load_sem.at[nx + 1])]
    for c in range(nx):
        cut = pl.ds(c * width, width)
        loads.append(pltpu.make_async_copy(snap_ref.at[0, :, cut], snap.at[:, cut], load_sem.at[c]))
    for load in loads:
        load.start()

    barrier = pltpu.get_barrier_semaphore()

    def greet(grp, core):
        pl.semaphore_signal(barrier, inc=1, device_id=(grp, core), device_id_type=MESH)

    greet(me, sibling)
    for d in range(1, nz):
        greet((zi + d) % nz * nplane + pi, rep)
    for d in range(1, nplane):
        greet(zi * nplane + (pi + d) % nplane, rep)
    pl.semaphore_wait(barrier, nz + nplane - 1)
    for d in range(1, nz):
        pl.semaphore_signal(
            word_sem, inc=1, device_id=((zi + d) % nz * nplane + pi, rep), device_id_type=MESH)
    pl.semaphore_signal(word_sem, inc=1, device_id=(me, sibling), device_id_type=MESH)

    ring = sorted(
        ((dx, dy) for dx in range(nx) for dy in range(ny)),
        key=lambda at: -min(at[0], nx - at[0]) - min(at[1], ny - at[1]))
    started = []

    def begin(copy):
        copy.start()
        started.append(copy)
        return copy

    def to_core(stage, src, dst):
        return [begin(pltpu.make_async_remote_copy(
            src_ref=src, dst_ref=dst, send_sem=core_s.at[stage], recv_sem=core_r.at[stage],
            device_id=(me, sibling), device_id_type=MESH))]

    def along_z(stage, src, dst):
        return [begin(pltpu.make_async_remote_copy(
            src_ref=src((zi + d) % nz), dst_ref=dst, send_sem=z_s.at[stage, d], recv_sem=z_r.at[stage, d],
            device_id=((zi + d) % nz * nplane + pi, rep), device_id_type=MESH)) for d in far(nz)[:-1]]

    def in_plane(stage, src, dst):
        copies = []
        for dx, dy in ring[:-1]:
            q = (pi // ny + dx) % nx * ny + (pi % ny + dy) % ny
            copies.append(begin(pltpu.make_async_remote_copy(
                src_ref=src(q), dst_ref=dst, send_sem=plane_s.at[stage, dx * ny + dy],
                recv_sem=plane_r.at[stage, dx * ny + dy],
                device_id=(zi * nplane + q, rep), device_id_type=MESH)))
        return copies

    def arrive(copies):
        for copy in copies:
            copy.wait_recv()

    def place(grp):
        z, x, y = grp // nplane, grp % nplane // ny, grp % ny
        return (x + z) % nx * block + z * (ny * 4) + y * 4

    def to_owner(stage, src, dst, grp, landed=0):
        return pltpu.make_async_remote_copy(
            src_ref=src, dst_ref=dst, send_sem=all_s.at[stage], recv_sem=all_r.at[landed],
            device_id=(grp, rep), device_id_type=MESH)

    zs = [(zi + d) % nz for d in far(nz)]
    xs = [(pi // ny + d) % nx for d in far(nx)]
    ys = [(pi % ny + d) % ny for d in far(ny)]

    loads[0].wait()
    ucut = jnp.concatenate(split(ufac[...].T), axis=0)
    core_copies = []
    for c in range(nx):
        loads[2 + c].wait()
        lo = c * width
        total = jnp.zeros((rank, width), F32)
        for k in range(0, rows, depth):
            high, low = split(snap[k:k + depth, lo:lo + width])
            shigh[k:k + depth, lo:lo + width] = high
            slow[k:k + depth, lo:lo + width] = low
            first = half(ucut[:, k:k + depth], high)
            total = total + (first[:rank] + (first[rank:] + half(ucut[:rank, k:k + depth], low)))
        for core in range(2):
            for z in range(nz):
                for k in range(tiles):
                    at = c * block + z * ny * 4 + k * 8
                    proj[core, at:at + 8, :] = total[core * rhalf + z * 8:core * rhalf + z * 8 + 8, k * 128:k * 128 + 128]
        cut = pl.ds(c * block, block)
        core_copies.append(to_core(c, proj.at[sibling, cut], other.at[cut]))

    pl.semaphore_wait(word_sem, nz)

    for c in range(nx):
        arrive(core_copies[c])
        at = c * block
        piece[at:at + block, :] = proj[rep, at:at + block, :] + other[at:at + block, :]

        for z in zs:
            for y in ys:
                x = (c + nx * nz - z) % nx
                copy = to_owner(
                    0, piece.at[pl.ds(at + z * (ny * 4) + y * 4, 4)], owned.at[pl.ds(me * 4, 4)], z * nplane + x * ny + y)
                if z is zs[-1] and y is ys[-1]:
                    pl.when(x != pi // ny)(copy.start)
                else:
                    copy.start()
    pltpu.make_async_copy(piece.at[pl.ds(place(me), 4)], owned.at[pl.ds(me * 4, 4)], all_r.at[0]).start()
    pltpu.make_async_copy(owned, owned, all_r.at[0]).wait()
    flat = jnp.concatenate([owned[pl.ds(c, count, stride=4), :] for c in range(4)], axis=1)

    loads[1].wait()
    tpart[...] = full(full(tfac[...], flat), flat, NT)
    trows = tpart.shape[0] // nz
    copies = along_z(PARTS, lambda q: tpart.at[pl.ds(q * trows, trows)], tz.at[zi])
    tz[zi] = tpart[pl.ds(zi * trows, trows), :]
    arrive(copies)
    tsum[...] = functools.reduce(jnp.add, [tz[k] for k in range(nz)])
    copies = in_plane(2 * PARTS, lambda q: tsum, tplane.at[rep, pi])
    for dx, dy in ring:
        q = (pi // ny + dx) % nx * ny + (pi % ny + dy) % ny
        copies.append(begin(pltpu.make_async_remote_copy(
            src_ref=tsum, dst_ref=tplane.at[rep, pi], send_sem=plane_s.at[2 * PARTS + 1, dx * ny + dy],
            recv_sem=plane_r.at[2 * PARTS + 1, dx * ny + dy], device_id=(zi * nplane + q, sibling),
            device_id_type=MESH)))
    tplane[rep, pi] = tsum[...]
    arrive(copies)
    tmine = pl.ds(zi * trows, trows)
    tall[tmine, :] = functools.reduce(jnp.add, [tplane[core, k] for core in range(2) for k in range(nplane)])
    arrive(along_z(PARTS + 1, lambda q: tall.at[tmine], tall.at[tmine]))
    start = tall[...]

    scale = 1.0 / jnp.sqrt(jnp.sum(start * start, axis=(0, 1), keepdims=True) + 1e-06)

    basis = start * scale
    for _ in range(STEPS):
        basis = 1.5 * basis - 0.5 * full(full(basis, basis, NT), basis)
    time_out[...] = basis * math.sqrt(count)
    mixed = full(full(basis.T, basis), flat)
    for c in range(4):
        wback[pl.ds(c, count, stride=4), :] = mixed[:, c * 128:(c + 1) * 128]

    spot = pl.ds(place(me), 4)

    my_part = (pi // ny + zi) % nx
    for z in zs:
        for x in xs:
            for y in ys:
                if not (z is zs[-1] and x is xs[-1] and y is ys[-1]):
                    grp = z * nplane + x * ny + y
                    to_owner(1, wback.at[pl.ds(grp * 4, 4)], wpieces.at[rep, spot], grp, 1 + my_part).start()
    pltpu.make_async_copy(wback.at[pl.ds(me * 4, 4)], wpieces.at[rep, spot], all_r.at[1 + my_part]).start()
    passed = []
    for c in range(nx):
        cut = pl.ds(c * block, block)
        pltpu.make_async_copy(wback.at[cut], wpieces.at[rep, cut], all_r.at[1 + c]).wait()
        passed.append(to_core(nx + c, wpieces.at[rep, cut], wpieces.at[rep, cut]))

    def narrowed(core, c):
        for m in range(nz // 2):
            for k in range(tiles):
                at = c * block + 2 * m * ny * 4 + k * 8
                both = jnp.concatenate(
                    [wpieces[core, at:at + 8, :], wpieces[core, at + ny * 4:at + ny * 4 + 8, :]], axis=0)
                high, low = split(both)
                row, lo = pl.ds(pl.multiple_of(core * rhalf + m * 16, 16), 16), c * width + k * 128
                wcut[row, lo:lo + 128] = high
                wcut[pl.ds(pl.multiple_of(rank + core * rhalf + m * 16, 16), 16), lo:lo + 128] = low

    for c in range(nx):
        narrowed(rep, c)
    for c in range(nx):
        arrive(passed[c])
        narrowed(sibling, c)

    part = rows // PARTS
    prows = part // nplane
    summed, crossed, spread = [], [], []
    for h in range(PARTS):
        for k in range(h * part, (h + 1) * part, min(part, 256)):
            high, low = shigh[k:k + min(part, 256), :], slow[k:k + min(part, 256), :]
            first = half(high, wcut[...], NT)
            prod[k:k + min(part, 256), :] = first[:, :rank] + (first[:, rank:] + half(low, wcut[:rank, :], NT))
        summed.append(in_plane(h, lambda q: prod.at[pl.ds(h * part + q * prows, prows)], pin.at[h, pi]))
        pin[h, pi] = prod[pl.ds(h * part + pi * prows, prows), :]
    for h in range(PARTS):
        arrive(summed[h])
        psum[h] = functools.reduce(jnp.add, [pin[h, k] for k in range(nplane)])
        crossed.append(along_z(h, lambda q: psum.at[h], pz.at[h, zi]))
        pz[h, zi] = psum[h]
    for h in range(PARTS):
        arrive(crossed[h])
        mine = pl.ds(h * part + pi * prows, prows)
        xall[mine, :] = functools.reduce(jnp.add, [pz[h, k] for k in range(nz)])
        spread.append(in_plane(PARTS + h, lambda q: xall.at[mine], xall.at[mine]))
    gram = jnp.zeros((rank, rank), F32)
    for h in range(PARTS):
        arrive(spread[h])
        some = xall[h * part:(h + 1) * part, :]
        gram = gram + full(some.T, some)
    gpart[...] = gram
    arrive(to_core(2 * nx, gpart, gother))
    gram = gpart[...] + gother[...]

    eye = jnp.where(
        lax.broadcasted_iota(jnp.int32, gram.shape, 0) == lax.broadcasted_iota(jnp.int32, gram.shape, 1), 1.0, 0.0
    ).astype(F32)
    norm = 1.0 / (jnp.sum(gram * eye, axis=(0, 1), keepdims=True) + 1e-06)
    inner, power = gram * norm, eye
    for _ in range(STEPS - 1):
        factor = 1.5 * eye - 0.5 * inner
        cut = thirds(factor)
        power = six(cut, thirds(power))
        inner = six(cut, thirds(six(cut, thirds(inner))))
    power = full(power, 1.5 * eye - 0.5 * inner)
    rows_out[...] = full(xall[...], power * (math.sqrt(2 * rows) * jnp.sqrt(norm)))
    for copy in started:
        copy.wait_send()
    rest = pl.ds(0, (count - 1) * 4)
    for stage in range(2):
        pltpu.make_async_copy(owned.at[rest], owned.at[rest], all_s.at[stage]).wait()


def solution(mesh):
    nz, nx, ny = dims = DIMS
    nplane = nx * ny
    count = nz * nplane

    def on_device(snapshots, row_factor, time_factor):
        _, rows, cols = snapshots.shape
        rank = row_factor.shape[1]
        modes = time_factor.shape[1]
        vmem = lambda *shape: pltpu.VMEM(shape, F32)
        narrow = lambda *shape: pltpu.VMEM(shape, BF16)
        sems = lambda *shape: pltpu.SemaphoreType.DMA(shape)
        part = rows // PARTS
        prows = part // nplane
        new_rows, new_time = pl.pallas_call(
            functools.partial(kernel, dims),
            out_shape=(
                jax.ShapeDtypeStruct((rows, rank), F32),
                jax.ShapeDtypeStruct((modes, count), F32),
            ),
            in_specs=[pl.BlockSpec(memory_space=pltpu.HBM)] * 3,
            out_specs=(pl.BlockSpec(memory_space=pltpu.VMEM),) * 2,
            scratch_shapes=[
                vmem(rows, cols), vmem(rows, rank), vmem(modes, count), narrow(rows, cols), narrow(rows, cols),
                vmem(2, count * 4, 128), vmem(count * 4, 128), vmem(count * 4, 128), vmem(count * 4, 128),
                vmem(modes, count), vmem(nz, modes // nz, count), vmem(modes // nz, count),
                vmem(2, nplane, modes // nz, count), vmem(modes, count),
                vmem(count * 4, 128), vmem(2, count * 4, 128),
                narrow(2 * rank, cols),
                vmem(rows, rank), vmem(PARTS, nplane, prows, rank), vmem(PARTS, prows, rank),
                vmem(PARTS, nz, prows, rank), vmem(rows, rank), vmem(rank, rank), vmem(rank, rank),
                sems(nx + 2), sems(2 * nx + 1), sems(2 * nx + 1), sems(2 * PARTS + 2, nplane), sems(2 * PARTS + 2, nplane),
                sems(PARTS + 2, nz), sems(PARTS + 2, nz), sems(2), sems(1 + nx), pltpu.SemaphoreType.REGULAR,
            ],
            compiler_params=pltpu.CompilerParams(
                collective_id=0, has_side_effects=True, vmem_limit_bytes=VMEM_MIB * 1024 * 1024),
        )(*(pltpu.with_memory_space_constraint(arg, pltpu.HBM) for arg in (snapshots, row_factor, time_factor.T)))
        return new_rows, new_time.T

    return jax.shard_map(
        on_device,
        mesh=mesh,
        in_specs=(P("grp", "rep", None), P("rep", None), P()),
        out_specs=(P("rep", None), P()),
        check_vma=False,
    )
```

```python
import functools
import math

import jax
import jax.numpy as jnp
from jax import lax
from jax.experimental import pallas as pl
from jax.experimental.pallas import tpu as pltpu
from jax.sharding import PartitionSpec as P

MESH = pl.DeviceIdType.MESH
STEPS = 8
DIMS = (8, 4, 4)
PARTS = 4
VMEM_MIB = 40
F32 = jnp.float32
BF16 = jnp.bfloat16
NN = (((1,), (0,)), ((), ()))
NT = (((1,), (1,)), ((), ()))


def full(left, right, dims=NN):
    return lax.dot_general(left, right, dims, precision=lax.Precision.HIGHEST, preferred_element_type=F32)


def half(left, right, dims=NN):
    return lax.dot_general(left, right, dims, preferred_element_type=F32)


def split(value):
    high = value.astype(BF16)
    return high, (value - high.astype(F32)).astype(BF16)


def thirds(value):
    high, rest = value.astype(BF16), value
    rest = rest - high.astype(F32)
    mid = rest.astype(BF16)
    return high, mid, (rest - mid.astype(F32)).astype(BF16)


def beside(*blocks):
    return jnp.concatenate(blocks, axis=1)


def above(*blocks):
    return jnp.concatenate(blocks, axis=0)


def six(left, right):
    high, mid, low = left
    rhigh, rmid, rlow = right
    n = rhigh.shape[1]
    four = half(beside(high, mid), above(beside(rhigh, rmid), beside(rmid, rhigh)))
    two = half(beside(high, low), above(rlow, rhigh))
    return four[:, :n] + (four[:, n:] + two)


def far(size):
    return sorted(range(size), key=lambda d: -min(d, size - d))


def kernel(dims, snap_ref, row_ref, time_ref, rows_out, time_out,
           snap, ufac, tfac, shigh, slow, proj, other, piece, owned,
           tpart, tz, tsum, tplane, tall,
           wback, wpieces, wcut,
           prod, pin, psum, pz, xall, gpart, gother,
           load_sem, core_s, core_r, plane_s, plane_r, z_s, z_r, all_s, all_r, team_s, team_r, sheet_s, sheet_r, word_sem):
    nz, nx, ny = dims
    nplane = nx * ny
    count = nz * nplane
    me = lax.axis_index("grp")
    rep = lax.axis_index("rep")
    zi, pi = me // nplane, me % nplane
    sibling = 1 - rep
    rank = ufac.shape[1]
    rhalf = rank // 2
    rows, cols = snap.shape
    tiles = ny // 2
    width = tiles * 128
    block = nz * ny * 4
    depth = min(rows, 256)

    loads = [pltpu.make_async_copy(row_ref, ufac, load_sem.at[nx]), pltpu.make_async_copy(time_ref, tfac, load_sem.at[nx + 1])]
    for c in range(nx):
        cut = pl.ds(c * width, width)
        loads.append(pltpu.make_async_copy(snap_ref.at[0, :, cut], snap.at[:, cut], load_sem.at[c]))
    for load in loads:
        load.start()

    barrier = pltpu.get_barrier_semaphore()

    def greet(grp, core):
        pl.semaphore_signal(barrier, inc=1, device_id=(grp, core), device_id_type=MESH)

    greet(me, sibling)
    for d in range(1, nz):
        greet((zi + d) % nz * nplane + pi, rep)
    for d in range(1, nplane):
        greet(zi * nplane + (pi + d) % nplane, rep)
    pl.semaphore_wait(barrier, nz + nplane - 1)
    for d in range(1, nz):
        pl.semaphore_signal(
            word_sem, inc=1, device_id=((zi + d) % nz * nplane + pi, rep), device_id_type=MESH)
    pl.semaphore_signal(word_sem, inc=1, device_id=(me, sibling), device_id_type=MESH)

    ring = sorted(
        ((dx, dy) for dx in range(nx) for dy in range(ny)),
        key=lambda at: -min(at[0], nx - at[0]) - min(at[1], ny - at[1]))
    started = []

    def begin(copy):
        copy.start()
        started.append(copy)
        return copy

    def to_core(stage, src, dst):
        return [begin(pltpu.make_async_remote_copy(
            src_ref=src, dst_ref=dst, send_sem=core_s.at[stage], recv_sem=core_r.at[stage],
            device_id=(me, sibling), device_id_type=MESH))]

    def along_z(stage, src, dst):
        return [begin(pltpu.make_async_remote_copy(
            src_ref=src((zi + d) % nz), dst_ref=dst, send_sem=z_s.at[stage, d], recv_sem=z_r.at[stage, d],
            device_id=((zi + d) % nz * nplane + pi, rep), device_id_type=MESH)) for d in far(nz)[:-1]]

    def in_plane(stage, src, dst):
        copies = []
        for dx, dy in ring[:-1]:
            q = (pi // ny + dx) % nx * ny + (pi % ny + dy) % ny
            copies.append(begin(pltpu.make_async_remote_copy(
                src_ref=src(q), dst_ref=dst, send_sem=plane_s.at[stage, dx * ny + dy],
                recv_sem=plane_r.at[stage, dx * ny + dy],
                device_id=(zi * nplane + q, rep), device_id_type=MESH)))
        return copies

    def arrive(copies):
        for copy in copies:
            copy.wait_recv()

    def place(grp):
        z, x, y = grp // nplane, grp % nplane // ny, grp % ny
        return (x + z) % nx * block + z * (ny * 4) + y * 4

    def to_owner(stage, src, dst, grp, landed=0):
        return pltpu.make_async_remote_copy(
            src_ref=src, dst_ref=dst, send_sem=all_s.at[stage], recv_sem=all_r.at[landed],
            device_id=(grp, rep), device_id_type=MESH)

    zs = [(zi + d) % nz for d in far(nz)]
    xs = [(pi // ny + d) % nx for d in far(nx)]
    ys = [(pi % ny + d) % ny for d in far(ny)]

    loads[0].wait()
    ucut = jnp.concatenate(split(ufac[...].T), axis=0)
    core_copies = []
    for c in range(nx):
        loads[2 + c].wait()
        lo = c * width
        total = jnp.zeros((rank, width), F32)
        for k in range(0, rows, depth):
            high, low = split(snap[k:k + depth, lo:lo + width])
            shigh[k:k + depth, lo:lo + width] = high
            slow[k:k + depth, lo:lo + width] = low
            first = half(ucut[:, k:k + depth], high)
            total = total + (first[:rank] + (first[rank:] + half(ucut[:rank, k:k + depth], low)))
        for core in range(2):
            for z in range(nz):
                for k in range(tiles):
                    at = c * block + z * ny * 4 + k * 8
                    proj[core, at:at + 8, :] = total[core * rhalf + z * 8:core * rhalf + z * 8 + 8, k * 128:k * 128 + 128]
        cut = pl.ds(c * block, block)
        core_copies.append(to_core(c, proj.at[sibling, cut], other.at[cut]))

    pl.semaphore_wait(word_sem, nz)

    for c in range(nx):
        arrive(core_copies[c])
        at = c * block
        piece[at:at + block, :] = proj[rep, at:at + block, :] + other[at:at + block, :]

        for z in zs:
            for y in ys:
                x = (c + nx * nz - z) % nx
                copy = to_owner(
                    0, piece.at[pl.ds(at + z * (ny * 4) + y * 4, 4)], owned.at[pl.ds(me * 4, 4)], z * nplane + x * ny + y)
                if z is zs[-1] and y is ys[-1]:
                    pl.when(x != pi // ny)(copy.start)
                else:
                    copy.start()
    pltpu.make_async_copy(piece.at[pl.ds(place(me), 4)], owned.at[pl.ds(me * 4, 4)], all_r.at[0]).start()
    pltpu.make_async_copy(owned, owned, all_r.at[0]).wait()
    flat = jnp.concatenate([owned[pl.ds(c, count, stride=4), :] for c in range(4)], axis=1)

    loads[1].wait()
    tpart[...] = full(full(tfac[...], flat), flat, NT)
    team = 2 * nx
    trows = tpart.shape[0] // team
    xi, yi = pi // ny, pi % ny
    mine = rep * nx + xi

    def in_team(stage, src, dst):
        copies = []
        for d in far(nx):
            for flip in (1, 0):
                if d or flip:
                    x, core = (xi + d) % nx, (sibling if flip else rep)
                    copies.append(begin(pltpu.make_async_remote_copy(
                        src_ref=src(core * nx + x), dst_ref=dst, send_sem=team_s.at[stage, flip * nx + d],
                        recv_sem=team_r.at[stage, flip * nx + d],
                        device_id=(zi * nplane + x * ny + yi, core), device_id_type=MESH)))
        return copies

    copies = in_team(0, lambda q: tpart.at[pl.ds(q * trows, trows)], tz.at[mine])
    tz[mine] = tpart[pl.ds(mine * trows, trows), :]
    arrive(copies)
    tsum[...] = functools.reduce(jnp.add, [tz[k] for k in range(team)])
    copies = []
    sheet = sorted(
        ((dz, dy) for dz in range(nz) for dy in range(ny)),
        key=lambda at: -min(at[0], nz - at[0]) - min(at[1], ny - at[1]))
    for dz, dy in sheet[:-1]:
        copies.append(begin(pltpu.make_async_remote_copy(
            src_ref=tsum, dst_ref=tplane.at[zi * ny + yi], send_sem=sheet_s.at[dz * ny + dy],
            recv_sem=sheet_r.at[dz * ny + dy],
            device_id=((zi + dz) % nz * nplane + xi * ny + (yi + dy) % ny, rep), device_id_type=MESH)))
    tplane[zi * ny + yi] = tsum[...]
    arrive(copies)
    tmine = pl.ds(mine * trows, trows)
    tall[tmine, :] = functools.reduce(jnp.add, [tplane[k] for k in range(nz * ny)])
    arrive(in_team(1, lambda q: tall.at[tmine], tall.at[tmine]))
    start = tall[...]

    scale = 1.0 / jnp.sqrt(jnp.sum(start * start, axis=(0, 1), keepdims=True) + 1e-06)

    basis = start * scale
    for _ in range(STEPS):
        basis = 1.5 * basis - 0.5 * full(full(basis, basis, NT), basis)
    time_out[...] = basis * math.sqrt(count)
    mixed = full(full(basis.T, basis), flat)
    for c in range(4):
        wback[pl.ds(c, count, stride=4), :] = mixed[:, c * 128:(c + 1) * 128]

    spot = pl.ds(place(me), 4)

    my_part = (pi // ny + zi) % nx
    for z in zs:
        for x in xs:
            for y in ys:
                if not (z is zs[-1] and x is xs[-1] and y is ys[-1]):
                    grp = z * nplane + x * ny + y
                    to_owner(1, wback.at[pl.ds(grp * 4, 4)], wpieces.at[rep, spot], grp, 1 + my_part).start()
    pltpu.make_async_copy(wback.at[pl.ds(me * 4, 4)], wpieces.at[rep, spot], all_r.at[1 + my_part]).start()
    passed = []
    for c in range(nx):
        cut = pl.ds(c * block, block)
        pltpu.make_async_copy(wback.at[cut], wpieces.at[rep, cut], all_r.at[1 + c]).wait()
        passed.append(to_core(nx + c, wpieces.at[rep, cut], wpieces.at[rep, cut]))

    def narrowed(core, c):
        for m in range(nz // 2):
            for k in range(tiles):
                at = c * block + 2 * m * ny * 4 + k * 8
                both = jnp.concatenate(
                    [wpieces[core, at:at + 8, :], wpieces[core, at + ny * 4:at + ny * 4 + 8, :]], axis=0)
                high, low = split(both)
                row, lo = pl.ds(pl.multiple_of(core * rhalf + m * 16, 16), 16), c * width + k * 128
                wcut[row, lo:lo + 128] = high
                wcut[pl.ds(pl.multiple_of(rank + core * rhalf + m * 16, 16), 16), lo:lo + 128] = low

    for c in range(nx):
        narrowed(rep, c)
    for c in range(nx):
        arrive(passed[c])
        narrowed(sibling, c)

    part = rows // PARTS
    prows = part // nplane
    summed, crossed, spread = [], [], []
    for h in range(PARTS):
        for k in range(h * part, (h + 1) * part, min(part, 256)):
            high, low = shigh[k:k + min(part, 256), :], slow[k:k + min(part, 256), :]
            first = half(high, wcut[...], NT)
            prod[k:k + min(part, 256), :] = first[:, :rank] + (first[:, rank:] + half(low, wcut[:rank, :], NT))
        summed.append(in_plane(h, lambda q: prod.at[pl.ds(h * part + q * prows, prows)], pin.at[h, pi]))
        pin[h, pi] = prod[pl.ds(h * part + pi * prows, prows), :]
    for h in range(PARTS):
        arrive(summed[h])
        psum[h] = functools.reduce(jnp.add, [pin[h, k] for k in range(nplane)])
        crossed.append(along_z(h, lambda q: psum.at[h], pz.at[h, zi]))
        pz[h, zi] = psum[h]
    for h in range(PARTS):
        arrive(crossed[h])
        mine = pl.ds(h * part + pi * prows, prows)
        xall[mine, :] = functools.reduce(jnp.add, [pz[h, k] for k in range(nz)])
        spread.append(in_plane(PARTS + h, lambda q: xall.at[mine], xall.at[mine]))
    gram = jnp.zeros((rank, rank), F32)
    for h in range(PARTS):
        arrive(spread[h])
        some = xall[h * part:(h + 1) * part, :]
        gram = gram + full(some.T, some)
    gpart[...] = gram
    arrive(to_core(2 * nx, gpart, gother))
    gram = gpart[...] + gother[...]

    eye = jnp.where(
        lax.broadcasted_iota(jnp.int32, gram.shape, 0) == lax.broadcasted_iota(jnp.int32, gram.shape, 1), 1.0, 0.0
    ).astype(F32)
    norm = 1.0 / (jnp.sum(gram * eye, axis=(0, 1), keepdims=True) + 1e-06)
    inner, power = gram * norm, eye
    for _ in range(STEPS - 1):
        factor = 1.5 * eye - 0.5 * inner
        cut = thirds(factor)
        power = six(cut, thirds(power))
        inner = six(cut, thirds(six(cut, thirds(inner))))
    power = full(power, 1.5 * eye - 0.5 * inner)
    rows_out[...] = full(xall[...], power * (math.sqrt(2 * rows) * jnp.sqrt(norm)))
    for copy in started:
        copy.wait_send()
    rest = pl.ds(0, (count - 1) * 4)
    for stage in range(2):
        pltpu.make_async_copy(owned.at[rest], owned.at[rest], all_s.at[stage]).wait()


def solution(mesh):
    nz, nx, ny = dims = DIMS
    nplane = nx * ny
    count = nz * nplane

    def on_device(snapshots, row_factor, time_factor):
        _, rows, cols = snapshots.shape
        rank = row_factor.shape[1]
        modes = time_factor.shape[1]
        vmem = lambda *shape: pltpu.VMEM(shape, F32)
        narrow = lambda *shape: pltpu.VMEM(shape, BF16)
        sems = lambda *shape: pltpu.SemaphoreType.DMA(shape)
        part = rows // PARTS
        prows = part // nplane
        new_rows, new_time = pl.pallas_call(
            functools.partial(kernel, dims),
            out_shape=(
                jax.ShapeDtypeStruct((rows, rank), F32),
                jax.ShapeDtypeStruct((modes, count), F32),
            ),
            in_specs=[pl.BlockSpec(memory_space=pltpu.HBM)] * 3,
            out_specs=(pl.BlockSpec(memory_space=pltpu.VMEM),) * 2,
            scratch_shapes=[
                vmem(rows, cols), vmem(rows, rank), vmem(modes, count), narrow(rows, cols), narrow(rows, cols),
                vmem(2, count * 4, 128), vmem(count * 4, 128), vmem(count * 4, 128), vmem(count * 4, 128),
                vmem(modes, count), vmem(2 * nx, modes // (2 * nx), count), vmem(modes // (2 * nx), count),
                vmem(nz * ny, modes // (2 * nx), count), vmem(modes, count),
                vmem(count * 4, 128), vmem(2, count * 4, 128),
                narrow(2 * rank, cols),
                vmem(rows, rank), vmem(PARTS, nplane, prows, rank), vmem(PARTS, prows, rank),
                vmem(PARTS, nz, prows, rank), vmem(rows, rank), vmem(rank, rank), vmem(rank, rank),
                sems(nx + 2), sems(2 * nx + 1), sems(2 * nx + 1), sems(2 * PARTS, nplane), sems(2 * PARTS, nplane),
                sems(PARTS, nz), sems(PARTS, nz), sems(2), sems(1 + nx),
                sems(2, 2 * nx), sems(2, 2 * nx), sems(nz * ny), sems(nz * ny), pltpu.SemaphoreType.REGULAR,
            ],
            compiler_params=pltpu.CompilerParams(
                collective_id=0, has_side_effects=True, vmem_limit_bytes=VMEM_MIB * 1024 * 1024),
        )(*(pltpu.with_memory_space_constraint(arg, pltpu.HBM) for arg in (snapshots, row_factor, time_factor.T)))
        return new_rows, new_time.T

    return jax.shard_map(
        on_device,
        mesh=mesh,
        in_specs=(P("grp", "rep", None), P("rep", None), P()),
        out_specs=(P("rep", None), P()),
        check_vma=False,
    )
```

```python
import functools
import math

import jax
import jax.numpy as jnp
from jax import lax
from jax.experimental import pallas as pl
from jax.experimental.pallas import tpu as pltpu
from jax.sharding import PartitionSpec as P

MESH = pl.DeviceIdType.MESH
STEPS = 8
DIMS = (8, 4, 4)
PARTS = 4
VMEM_MIB = 40
F32 = jnp.float32
BF16 = jnp.bfloat16
NN = (((1,), (0,)), ((), ()))
NT = (((1,), (1,)), ((), ()))


def full(left, right, dims=NN):
    return lax.dot_general(left, right, dims, precision=lax.Precision.HIGHEST, preferred_element_type=F32)


def half(left, right, dims=NN):
    return lax.dot_general(left, right, dims, preferred_element_type=F32)


def split(value):
    high = value.astype(BF16)
    return high, (value - high.astype(F32)).astype(BF16)


def thirds(value):
    high, rest = value.astype(BF16), value
    rest = rest - high.astype(F32)
    mid = rest.astype(BF16)
    return high, mid, (rest - mid.astype(F32)).astype(BF16)


def beside(*blocks):
    return jnp.concatenate(blocks, axis=1)


def above(*blocks):
    return jnp.concatenate(blocks, axis=0)


def six(left, right):
    high, mid, low = left
    rhigh, rmid, rlow = right
    n = rhigh.shape[1]
    four = half(beside(high, mid), above(beside(rhigh, rmid), beside(rmid, rhigh)))
    two = half(beside(high, low), above(rlow, rhigh))
    return four[:, :n] + (four[:, n:] + two)


def far(size):
    return sorted(range(size), key=lambda d: -min(d, size - d))


def kernel(dims, snap_ref, row_ref, time_ref, rows_out, time_out,
           snap, ufac, tfac, shigh, slow, proj, other, piece, owned,
           tpart, tz, tsum, tplane, tall,
           wback, wpieces, wcut,
           prod, pin, psum, pz, xall, gpart, gother,
           load_sem, core_s, core_r, plane_s, plane_r, z_s, z_r, all_s, all_r, team_s, team_r, sheet_s, sheet_r, word_sem):
    nz, nx, ny = dims
    nplane = nx * ny
    count = nz * nplane
    me = lax.axis_index("grp")
    rep = lax.axis_index("rep")
    zi, pi = me // nplane, me % nplane
    sibling = 1 - rep
    rank = ufac.shape[1]
    rhalf = rank // 2
    rows, cols = snap.shape
    tiles = ny // 2
    width = tiles * 128
    block = nz * ny * 4
    depth = min(rows, 256)

    loads = [pltpu.make_async_copy(row_ref, ufac, load_sem.at[nx]), pltpu.make_async_copy(time_ref, tfac, load_sem.at[nx + 1])]
    for c in range(nx):
        cut = pl.ds(c * width, width)
        loads.append(pltpu.make_async_copy(snap_ref.at[0, :, cut], snap.at[:, cut], load_sem.at[c]))
    for load in loads:
        load.start()

    barrier = pltpu.get_barrier_semaphore()

    def greet(grp, core):
        pl.semaphore_signal(barrier, inc=1, device_id=(grp, core), device_id_type=MESH)

    greet(me, sibling)
    for d in range(1, nz):
        greet((zi + d) % nz * nplane + pi, rep)
    for d in range(1, nplane):
        greet(zi * nplane + (pi + d) % nplane, rep)
    pl.semaphore_wait(barrier, nz + nplane - 1)
    for d in range(1, nz):
        pl.semaphore_signal(
            word_sem, inc=1, device_id=((zi + d) % nz * nplane + pi, rep), device_id_type=MESH)
    pl.semaphore_signal(word_sem, inc=1, device_id=(me, sibling), device_id_type=MESH)

    ring = sorted(
        ((dx, dy) for dx in range(nx) for dy in range(ny)),
        key=lambda at: -min(at[0], nx - at[0]) - min(at[1], ny - at[1]))
    started = []

    def begin(copy):
        copy.start()
        started.append(copy)
        return copy

    def to_core(stage, src, dst):
        return [begin(pltpu.make_async_remote_copy(
            src_ref=src, dst_ref=dst, send_sem=core_s.at[stage], recv_sem=core_r.at[stage],
            device_id=(me, sibling), device_id_type=MESH))]

    def along_z(stage, src, dst):
        return [begin(pltpu.make_async_remote_copy(
            src_ref=src((zi + d) % nz), dst_ref=dst, send_sem=z_s.at[stage, d], recv_sem=z_r.at[stage, d],
            device_id=((zi + d) % nz * nplane + pi, rep), device_id_type=MESH)) for d in far(nz)[:-1]]

    def in_plane(stage, src, dst):
        copies = []
        for dx, dy in ring[:-1]:
            q = (pi // ny + dx) % nx * ny + (pi % ny + dy) % ny
            copies.append(begin(pltpu.make_async_remote_copy(
                src_ref=src(q), dst_ref=dst, send_sem=plane_s.at[stage, dx * ny + dy],
                recv_sem=plane_r.at[stage, dx * ny + dy],
                device_id=(zi * nplane + q, rep), device_id_type=MESH)))
        return copies

    def arrive(copies):
        for copy in copies:
            copy.wait_recv()

    def place(grp):
        z, x, y = grp // nplane, grp % nplane // ny, grp % ny
        return (x + z) % nx * block + z * (ny * 4) + y * 4

    def to_owner(stage, src, dst, grp, landed=0):
        return pltpu.make_async_remote_copy(
            src_ref=src, dst_ref=dst, send_sem=all_s.at[stage], recv_sem=all_r.at[landed],
            device_id=(grp, rep), device_id_type=MESH)

    zs = [(zi + d) % nz for d in far(nz)]
    xs = [(pi // ny + d) % nx for d in far(nx)]
    ys = [(pi % ny + d) % ny for d in far(ny)]

    loads[0].wait()
    ucut = jnp.concatenate(split(ufac[...].T), axis=0)
    core_copies = []
    for c in range(nx):
        loads[2 + c].wait()
        lo = c * width
        total = jnp.zeros((rank, width), F32)
        for k in range(0, rows, depth):
            high, low = split(snap[k:k + depth, lo:lo + width])
            shigh[k:k + depth, lo:lo + width] = high
            slow[k:k + depth, lo:lo + width] = low
            first = half(ucut[:, k:k + depth], high)
            total = total + (first[:rank] + (first[rank:] + half(ucut[:rank, k:k + depth], low)))
        for core in range(2):
            for z in range(nz):
                for k in range(tiles):
                    at = c * block + z * ny * 4 + k * 8
                    proj[core, at:at + 8, :] = total[core * rhalf + z * 8:core * rhalf + z * 8 + 8, k * 128:k * 128 + 128]
        cut = pl.ds(c * block, block)
        core_copies.append(to_core(c, proj.at[sibling, cut], other.at[cut]))

    pl.semaphore_wait(word_sem, nz)

    for c in range(nx):
        arrive(core_copies[c])
        at = c * block
        piece[at:at + block, :] = proj[rep, at:at + block, :] + other[at:at + block, :]

        for z in zs:
            for y in ys:
                x = (c + nx * nz - z) % nx
                copy = to_owner(
                    0, piece.at[pl.ds(at + z * (ny * 4) + y * 4, 4)], owned.at[pl.ds(me * 4, 4)], z * nplane + x * ny + y)
                if z is zs[-1] and y is ys[-1]:
                    pl.when(x != pi // ny)(copy.start)
                else:
                    copy.start()
    pltpu.make_async_copy(piece.at[pl.ds(place(me), 4)], owned.at[pl.ds(me * 4, 4)], all_r.at[0]).start()
    pltpu.make_async_copy(owned, owned, all_r.at[0]).wait()
    flat = jnp.concatenate([owned[pl.ds(c, count, stride=4), :] for c in range(4)], axis=1)

    loads[1].wait()
    tpart[...] = full(full(tfac[...], flat), flat, NT)
    team = 2 * nx
    trows = tpart.shape[0] // team
    xi, yi = pi // ny, pi % ny
    mine = rep * nx + xi

    def in_team(stage, src, dst):
        copies = []
        for d in far(nx):
            for flip in (1, 0):
                if d or flip:
                    x, core = (xi + d) % nx, (sibling if flip else rep)
                    copies.append(begin(pltpu.make_async_remote_copy(
                        src_ref=src(core * nx + x), dst_ref=dst, send_sem=team_s.at[stage, flip * nx + d],
                        recv_sem=team_r.at[stage, flip * nx + d],
                        device_id=(zi * nplane + x * ny + yi, core), device_id_type=MESH)))
        return copies

    copies = in_team(0, lambda q: tpart.at[pl.ds(q * trows, trows)], tz.at[mine])
    tz[mine] = tpart[pl.ds(mine * trows, trows), :]
    arrive(copies)
    tsum[...] = functools.reduce(jnp.add, [tz[k] for k in range(team)])
    copies = []
    sheet = sorted(
        ((dz, dy) for dz in range(nz) for dy in range(ny)),
        key=lambda at: -min(at[0], nz - at[0]) - min(at[1], ny - at[1]))
    for dz, dy in sheet[:-1]:
        copies.append(begin(pltpu.make_async_remote_copy(
            src_ref=tsum, dst_ref=tplane.at[zi * ny + yi], send_sem=sheet_s.at[dz * ny + dy],
            recv_sem=sheet_r.at[dz * ny + dy],
            device_id=((zi + dz) % nz * nplane + xi * ny + (yi + dy) % ny, rep), device_id_type=MESH)))
    tplane[zi * ny + yi] = tsum[...]
    arrive(copies)
    tmine = pl.ds(mine * trows, trows)
    tall[tmine, :] = functools.reduce(jnp.add, [tplane[k] for k in range(nz * ny)])
    arrive(in_team(1, lambda q: tall.at[tmine], tall.at[tmine]))
    start = tall[...]

    scale = 1.0 / jnp.sqrt(jnp.sum(start * start, axis=(0, 1), keepdims=True) + 1e-06)

    basis = start * scale
    for _ in range(STEPS):
        basis = 1.5 * basis - 0.5 * full(full(basis, basis, NT), basis)
    time_out[...] = basis * math.sqrt(count)
    mixed = full(full(basis.T, basis), flat)
    for c in range(4):
        wback[pl.ds(c, count, stride=4), :] = mixed[:, c * 128:(c + 1) * 128]

    spot = pl.ds(place(me), 4)

    my_part = (pi // ny + zi) % nx
    for z in zs:
        for x in xs:
            for y in ys:
                if not (z is zs[-1] and x is xs[-1] and y is ys[-1]):
                    grp = z * nplane + x * ny + y
                    to_owner(1, wback.at[pl.ds(grp * 4, 4)], wpieces.at[rep, spot], grp, 1 + my_part).start()
    pltpu.make_async_copy(wback.at[pl.ds(me * 4, 4)], wpieces.at[rep, spot], all_r.at[1 + my_part]).start()
    passed = []
    for c in range(nx):
        cut = pl.ds(c * block, block)
        pltpu.make_async_copy(wback.at[cut], wpieces.at[rep, cut], all_r.at[1 + c]).wait()
        passed.append(to_core(nx + c, wpieces.at[rep, cut], wpieces.at[rep, cut]))

    def narrowed(core, c):
        for m in range(nz // 2):
            for k in range(tiles):
                at = c * block + 2 * m * ny * 4 + k * 8
                both = jnp.concatenate(
                    [wpieces[core, at:at + 8, :], wpieces[core, at + ny * 4:at + ny * 4 + 8, :]], axis=0)
                high, low = split(both)
                row, lo = pl.ds(pl.multiple_of(core * rhalf + m * 16, 16), 16), c * width + k * 128
                wcut[row, lo:lo + 128] = high
                wcut[pl.ds(pl.multiple_of(rank + core * rhalf + m * 16, 16), 16), lo:lo + 128] = low

    for c in range(nx):
        narrowed(rep, c)
    for c in range(nx):
        arrive(passed[c])
        narrowed(sibling, c)

    part = rows // PARTS
    prows = part // nplane
    summed, crossed, spread = [], [], []
    early = list(started)
    for h in range(PARTS):
        for k in range(h * part, (h + 1) * part, min(part, 256)):
            high, low = shigh[k:k + min(part, 256), :], slow[k:k + min(part, 256), :]
            first = half(high, wcut[...], NT)
            prod[k:k + min(part, 256), :] = first[:, :rank] + (first[:, rank:] + half(low, wcut[:rank, :], NT))
        summed.append(in_plane(h, lambda q: prod.at[pl.ds(h * part + q * prows, prows)], pin.at[h, pi]))
        pin[h, pi] = prod[pl.ds(h * part + pi * prows, prows), :]
    for h in range(PARTS):
        arrive(summed[h])
        psum[h] = functools.reduce(jnp.add, [pin[h, k] for k in range(nplane)])
        crossed.append(along_z(h, lambda q: psum.at[h], pz.at[h, zi]))
        pz[h, zi] = psum[h]
    for h in range(PARTS):
        arrive(crossed[h])
        mine = pl.ds(h * part + pi * prows, prows)
        xall[mine, :] = functools.reduce(jnp.add, [pz[h, k] for k in range(nz)])
        spread.append(in_plane(PARTS + h, lambda q: xall.at[mine], xall.at[mine]))
    for copy in early + [copy for copies in summed + crossed for copy in copies]:
        copy.wait_send()
    rest = pl.ds(0, (count - 1) * 4)
    for stage in range(2):
        pltpu.make_async_copy(owned.at[rest], owned.at[rest], all_s.at[stage]).wait()
    gram = jnp.zeros((rank, rank), F32)
    for h in range(PARTS):
        arrive(spread[h])
        some = xall[h * part:(h + 1) * part, :]
        gram = gram + full(some.T, some)
    gpart[...] = gram
    swap = to_core(2 * nx, gpart, gother)
    for copies in spread:
        for copy in copies:
            copy.wait_send()
    arrive(swap)
    gram = gpart[...] + gother[...]

    eye = jnp.where(
        lax.broadcasted_iota(jnp.int32, gram.shape, 0) == lax.broadcasted_iota(jnp.int32, gram.shape, 1), 1.0, 0.0
    ).astype(F32)
    norm = 1.0 / (jnp.sum(gram * eye, axis=(0, 1), keepdims=True) + 1e-06)
    inner, power = gram * norm, eye
    for _ in range(STEPS - 1):
        factor = 1.5 * eye - 0.5 * inner
        cut = thirds(factor)
        power = six(cut, thirds(power))
        inner = six(cut, thirds(six(cut, thirds(inner))))
    power = full(power, 1.5 * eye - 0.5 * inner)
    rows_out[...] = full(xall[...], power * (math.sqrt(2 * rows) * jnp.sqrt(norm)))
    for copy in swap:
        copy.wait_send()


def solution(mesh):
    nz, nx, ny = dims = DIMS
    nplane = nx * ny
    count = nz * nplane

    def on_device(snapshots, row_factor, time_factor):
        _, rows, cols = snapshots.shape
        rank = row_factor.shape[1]
        modes = time_factor.shape[1]
        vmem = lambda *shape: pltpu.VMEM(shape, F32)
        narrow = lambda *shape: pltpu.VMEM(shape, BF16)
        sems = lambda *shape: pltpu.SemaphoreType.DMA(shape)
        part = rows // PARTS
        prows = part // nplane
        new_rows, new_time = pl.pallas_call(
            functools.partial(kernel, dims),
            out_shape=(
                jax.ShapeDtypeStruct((rows, rank), F32),
                jax.ShapeDtypeStruct((modes, count), F32),
            ),
            in_specs=[pl.BlockSpec(memory_space=pltpu.HBM)] * 3,
            out_specs=(pl.BlockSpec(memory_space=pltpu.VMEM),) * 2,
            scratch_shapes=[
                vmem(rows, cols), vmem(rows, rank), vmem(modes, count), narrow(rows, cols), narrow(rows, cols),
                vmem(2, count * 4, 128), vmem(count * 4, 128), vmem(count * 4, 128), vmem(count * 4, 128),
                vmem(modes, count), vmem(2 * nx, modes // (2 * nx), count), vmem(modes // (2 * nx), count),
                vmem(nz * ny, modes // (2 * nx), count), vmem(modes, count),
                vmem(count * 4, 128), vmem(2, count * 4, 128),
                narrow(2 * rank, cols),
                vmem(rows, rank), vmem(PARTS, nplane, prows, rank), vmem(PARTS, prows, rank),
                vmem(PARTS, nz, prows, rank), vmem(rows, rank), vmem(rank, rank), vmem(rank, rank),
                sems(nx + 2), sems(2 * nx + 1), sems(2 * nx + 1), sems(2 * PARTS, nplane), sems(2 * PARTS, nplane),
                sems(PARTS, nz), sems(PARTS, nz), sems(2), sems(1 + nx),
                sems(2, 2 * nx), sems(2, 2 * nx), sems(nz * ny), sems(nz * ny), pltpu.SemaphoreType.REGULAR,
            ],
            compiler_params=pltpu.CompilerParams(
                collective_id=0, has_side_effects=True, vmem_limit_bytes=VMEM_MIB * 1024 * 1024),
        )(*(pltpu.with_memory_space_constraint(arg, pltpu.HBM) for arg in (snapshots, row_factor, time_factor.T)))
        return new_rows, new_time.T

    return jax.shard_map(
        on_device,
        mesh=mesh,
        in_specs=(P("grp", "rep", None), P("rep", None), P()),
        out_specs=(P("rep", None), P()),
        check_vma=False,
    )
```
